256 devices in a mesh: row: 16 (over z_hi, y, core), col: 16 (over z_lo, x).
Axes of the slice: x: 4, y: 4, z: 8 (z_hi: 2, z_lo: 4; z = z_hi * 4 + z_lo), core: 2. Of those that a mesh axis runs over, the one named last changes fastest.
Arguments:
- tokens: bfloat16 [2048, 8192], P('col', 'row'), may hold values from -6 to 6
- gate_vals: bfloat16 [448, 64, 4096], P('col', 'row'), may hold values from -0.09375 to 0.09375
- gate_scales: float32 [448, 64], P('col', 'row'), may hold values from 0.3 to 3
- gate_rows: int32 [448, 64], P('col', 'row'), may hold values from 0 to 127, as said below
- up_vals: bfloat16 [448, 64, 4096], P('col', 'row'), may hold values from -0.09375 to 0.09375
- up_scales: float32 [448, 64], P('col', 'row'), may hold values from 0.3 to 3
- up_rows: int32 [448, 64], P('col', 'row'), may hold values from 0 to 127, as said below
- down_vals: bfloat16 [128, 224, 4096], P('row', 'col'), may hold values from -0.046875 to 0.046875
- down_scales: float32 [128, 224], P('row', 'col'), may hold values from 0.3 to 3
- down_rows: int32 [128, 224], P('row', 'col'), may hold values from 0 to 447, as said below
Outputs:
- mixed: bfloat16 [2048, 8192], P('col', 'row')
The draws below stay inside these ranges and needn't reach their ends.
Inputs may be any that keep to these rules, and one draw needn't show every extreme that they name: Row j of gate_rows holds distinct block rows; slots k with the same k // 4 hold exactly half of the block rows from (k // 4) * 8 to that plus 8 - 1, in increasing order. `up_rows`: same law as gate_rows, drawn independently. Row j of down_rows holds distinct block rows of the hidden units; slots k with the same k // 14 hold exactly half of the block rows from (k // 14) * 28 to that plus 28 - 1, in increasing order.
All inputs are finite; a program needn't handle non-finite values.
Results may differ from the reference program's by a relative error of at most 0.03.
Values may be sent and summed in bfloat16 or wider, within the bound.
A program may use at most 128 MiB of HBM per device.

```python
import math
import jax
import jax.numpy as jnp
from jax import lax

D = 8192
FF = 28672
BLOCK = 64
TOKENS = 2048
GROUP = 8
GFF = 28
FF_BLOCKS = 448
KEPT = 64
D_BLOCKS = 128
KEPT_FF = 224
N_ROW = 16
N_COL = 16


def pick_rows(key, columns, members, group_size):
    base = jnp.broadcast_to(jnp.arange(group_size, dtype=jnp.int32), (columns, members, group_size))
    shuffled = jax.random.permutation(key, base, axis=2, independent=True)
    chosen = jnp.sort(shuffled[:, :, :group_size // 2], axis=2)
    chosen = chosen + (jnp.arange(members, dtype=jnp.int32) * group_size)[None, :, None]
    return chosen.reshape(columns, members * (group_size // 2)).astype(jnp.int32)


def draw_gate_rows(key, part):
    return pick_rows(jax.random.fold_in(key, 11), FF_BLOCKS, D // (BLOCK * GROUP), GROUP)


def draw_up_rows(key, part):
    return pick_rows(jax.random.fold_in(key, 23), FF_BLOCKS, D // (BLOCK * GROUP), GROUP)


def draw_down_rows(key, part):
    return pick_rows(jax.random.fold_in(key, 37), D_BLOCKS, FF // (BLOCK * GFF), GFF)


def levels(own_key, dims, pieces, least, largest):
    gain, own = 1.0, jax.random.fold_in(own_key, 6)
    for dim, shards_of in pieces:
        heights = jnp.exp(jax.random.uniform(jax.random.fold_in(own, dim), (shards_of,), jnp.float32, least / len(pieces), largest / len(pieces)))
        gain = gain * jnp.repeat(heights, dims[dim] // shards_of).reshape([-1 if axis == dim else 1 for axis in range(len(dims))])
    return gain


def scatter_about(own_key, dims, deviation, most, pieces=(), kind=jnp.bfloat16):
    entries = deviation * jax.random.normal(own_key, dims, jnp.float32)
    if pieces:
        entries = entries * levels(own_key, dims, pieces, -0.22, 0.18)
    return jnp.clip(entries, -most, most).astype(kind)


def setup_inputs(seed: int = 0) -> dict:
    key_list = jax.random.split(jax.random.key(seed), 11)
    tokens = scatter_about(key_list[0], (TOKENS, D), 1.0, 6.0, ((0, 16), (1, 16)))
    gate_vals = scatter_about(key_list[1], (FF_BLOCKS, KEPT, BLOCK * BLOCK), (D // 2) ** -0.5, 0.09375, ((0, 16), (1, 16)))
    gate_scales = jnp.clip(jnp.exp(math.log(3.0) - 2.3025851 * jax.random.uniform(key_list[2], (FF_BLOCKS, KEPT), jnp.float32) ** levels(key_list[2], (FF_BLOCKS, KEPT), ((0, 16), (1, 16)), -0.2, 0.2)), 0.3, 3.0)
    gate_rows = draw_gate_rows(jax.random.fold_in(key_list[10], 71), 0)
    up_vals = scatter_about(key_list[4], (FF_BLOCKS, KEPT, BLOCK * BLOCK), (D // 2) ** -0.5, 0.09375, ((0, 16), (1, 16)))
    up_scales = jnp.clip(jnp.exp(math.log(3.0) - 2.3025851 * jax.random.uniform(key_list[5], (FF_BLOCKS, KEPT), jnp.float32) ** levels(key_list[5], (FF_BLOCKS, KEPT), ((0, 16), (1, 16)), -0.2, 0.2)), 0.3, 3.0)
    up_rows = draw_up_rows(jax.random.fold_in(key_list[10], 71), 0)
    down_vals = scatter_about(key_list[7], (D_BLOCKS, KEPT_FF, BLOCK * BLOCK), (FF // 2) ** -0.5, 0.046875, ((0, 16), (1, 16)))
    down_scales = jnp.clip(jnp.exp(math.log(3.0) - 2.3025851 * jax.random.uniform(key_list[8], (D_BLOCKS, KEPT_FF), jnp.float32) ** levels(key_list[8], (D_BLOCKS, KEPT_FF), ((0, 16), (1, 16)), -0.2, 0.2)), 0.3, 3.0)
    down_rows = draw_down_rows(jax.random.fold_in(key_list[10], 71), 0)
    return {"tokens": tokens, "gate_vals": gate_vals, "gate_scales": gate_scales, "gate_rows": gate_rows, "up_vals": up_vals, "up_scales": up_scales, "up_rows": up_rows, "down_vals": down_vals, "down_scales": down_scales, "down_rows": down_rows}


def rounded(values):
    return lax.optimization_barrier(values.astype(jnp.bfloat16)).astype(jnp.float32)


def dense_panel(values, scales, indices, offset, groups):
    blocks = rounded(values.astype(jnp.float32) * scales[:, :, None])
    onehot = (indices[:, :, None] - offset == jnp.arange(groups, dtype=jnp.int32)[None, None, :]).astype(jnp.float32)
    matrix = jnp.einsum("jkg,jkc->gjc", onehot, blocks, precision=lax.Precision.HIGHEST)
    matrix = matrix.reshape(groups, values.shape[0], BLOCK, BLOCK).transpose(0, 2, 1, 3)
    return matrix.reshape(groups * BLOCK, values.shape[0] * BLOCK)


def grouped_product(inputs, values, scales, indices, members, groups):
    kept_each = values.shape[1] // members
    columns = inputs.shape[1] // members
    running = jnp.zeros((inputs.shape[0], values.shape[0] * BLOCK), jnp.float32)
    for member in range(members):
        matrix = dense_panel(values[:, member * kept_each:(member + 1) * kept_each],
                             scales[:, member * kept_each:(member + 1) * kept_each],
                             indices[:, member * kept_each:(member + 1) * kept_each],
                             member * groups, groups)
        partial_value = jnp.dot(inputs[:, member * columns:(member + 1) * columns].astype(jnp.float32), matrix,
                          precision=lax.Precision.HIGHEST, preferred_element_type=jnp.float32)
        running = running + rounded(partial_value)
    return running


def reference(tokens, gate_vals, gate_scales, gate_rows, up_vals, up_scales, up_rows, down_vals, down_scales, down_rows):
    gate = grouped_product(tokens, gate_vals, gate_scales, gate_rows, N_ROW, GROUP)
    up = grouped_product(tokens, up_vals, up_scales, up_rows, N_ROW, GROUP)
    hidden = (jax.nn.silu(gate) * up).astype(jnp.bfloat16)
    mixed = grouped_product(hidden, down_vals, down_scales, down_rows, N_COL, GFF)
    return mixed.astype(jnp.bfloat16)
```

```python
import jax
import jax.numpy as jnp
from jax import lax
from jax.experimental import pallas as pl
from jax.experimental.pallas import tpu as pltpu
from jax.sharding import PartitionSpec as P

BF = jnp.bfloat16
F32 = jnp.float32
MESH = pl.DeviceIdType.MESH
NCH = 7
PIECES = ((0, 512, 8), (512, 256, 4), (768, 128, 2))


def mult(v, m):
    return pl.multiple_of(v, m)


def order_matrix(width, members):
    src = lax.broadcasted_iota(jnp.int32, (width, width), 0)
    k = lax.broadcasted_iota(jnp.int32, (width, width), 1)
    rl = lax.rem(k, members)
    hi = lax.div(k, members)
    i = lax.rem(hi, 32)
    h = lax.div(hi, 32)
    return jnp.where(src == rl * 64 + 2 * i + h, 1.0, 0.0).astype(BF)


def kernel(
    tok, comb, draw, tabs, tabd, out,
    x_all, tst, p512, wr, tb, dr, td, panel,
    own, bsend, brecv, own2, zsend, zrecv, hn, hid, wd, acc,
    o1s, o1r, o2s, o2r, own3, o3s,
    sem_t, sem_tx, sem_ws, sem_wr, sem_d, sem_b, sem_z, sem_hs, sem_hr, sem_o1, sem_o2, sem_o3,
):
    row = lax.axis_index("row")
    col = lax.axis_index("col")
    core = lax.rem(row, 2)
    y = lax.rem(lax.div(row, 2), 4)
    zh = lax.div(row, 8)
    x = lax.rem(col, 4)
    zl = lax.div(col, 4)
    b = lax.div(y, 2)
    kp = lax.rem(y, 2)
    a = lax.rem(lax.div(y + 1, 2), 2)
    g = core * 2 + kp
    sib = (row + 1 - 2 * core, col)
    row_a = row + 2 - 4 * kp
    dev_a = (row_a, col)
    dev_aa = (row_a + 1 - 2 * core, col)
    dev_b = (zh * 8 + (3 - y) * 2 + core, col)
    dev_z = ((1 - zh) * 8 + y * 2 + core, col)

    def xdev(d):
        return (row, zl * 4 + lax.rem(x + d, 4))

    def zdev(d):
        return (row, lax.rem(zl + d, 4) * 4 + x)

    def remote(src, dst, ss, rs, dev):
        return pltpu.make_async_remote_copy(
            src_ref=src, dst_ref=dst, send_sem=ss, recv_sem=rs, device_id=dev, device_id_type=MESH
        )

    def arrived(ref, sem):
        pltpu.make_async_copy(ref, ref, sem).wait()

    barrier = pltpu.get_barrier_semaphore()
    partners = [sib, dev_a, dev_aa, dev_b, dev_z] + [xdev(d) for d in (1, 2, 3)] + [zdev(d) for d in (1, 2, 3)]
    for dev in partners:
        pl.semaphore_signal(barrier, inc=1, device_id=dev, device_id_type=MESH)

    p512[...] = order_matrix(512, 8)
    tst[...] = jnp.dot(tok[...], p512[...], preferred_element_type=F32).astype(BF)
    myrow = mult((x * 4 + zl) * 64, 64)
    mylane = mult(core * 1024 + kp * 512, 512)
    corelane = mult(core * 1024, 1024)
    x_all[pl.ds(myrow, 64), pl.ds(mylane, 512)] = tst[pl.ds(mult(a * 64, 64), 64), :]

    pl.semaphore_wait(barrier, len(partners))

    sends = []

    def go(copy):
        copy.start()
        sends.append(copy)

    go(remote(tst.at[pl.ds(mult((1 - a) * 64, 64), 64), :],
              x_all.at[pl.ds(myrow, 64), pl.ds(mylane, 512)], sem_t.at[0, 0], sem_t.at[1, 0], dev_a))
    wdests = ((dev_a, core), (dev_aa, 1 - core), (sib, 1 - core))
    for n, (dev, half) in enumerate(wdests):
        go(remote(tabs.at[half], tb.at[g], sem_ws.at[8, n], sem_wr.at[8, g], dev))
    pltpu.make_async_copy(tabs.at[core], tb.at[g], sem_wr.at[8, g]).start()
    for p in range(NCH):
        for n, (dev, half) in enumerate(wdests):
            go(remote(comb.at[half * NCH + p], wr.at[p, g], sem_ws.at[p, n], sem_wr.at[p, g], dev))
        pltpu.make_async_copy(comb.at[core * NCH + p], wr.at[p, g], sem_wr.at[p, g]).start()
    go(remote(tabd, td.at[kp], sem_d.at[0, 0], sem_d.at[2, kp], dev_a))
    pltpu.make_async_copy(tabd, td.at[kp], sem_d.at[2, kp]).start()
    go(remote(draw, dr.at[kp], sem_d.at[0, 1], sem_d.at[1, kp], dev_a))
    pltpu.make_async_copy(draw, dr.at[kp], sem_d.at[1, kp]).start()

    def block(xs, zs):
        return x_all.at[pl.ds(mult((xs * 4 + zs) * 64, 64), 64), pl.ds(corelane, 1024)]

    def quarter(xs):
        return x_all.at[pl.ds(mult(xs * 256, 256), 256), pl.ds(corelane, 1024)]

    other = mult(core * 1024 + (1 - kp) * 512, 512)
    arrived(x_all.at[pl.ds(myrow, 64), pl.ds(other, 512)], sem_t.at[1, 0])
    for d in (1, 2, 3):
        go(remote(block(x, zl), block(x, zl), sem_t.at[0, d], sem_t.at[1, d], zdev(d)))
    for d in (2, 1, 3):
        go(remote(block(x, zl), block(x, zl), sem_tx.at[0, d, 0], sem_tx.at[1, d, 0], xdev(d)))
    for dz in (1, 3, 2):
        zs = lax.rem(zl + 4 - dz, 4)
        arrived(block(x, zs), sem_t.at[1, dz])
        for d in (2, 1, 3):
            go(remote(block(x, zs), block(x, zs), sem_tx.at[0, d, dz], sem_tx.at[1, d, dz], xdev(d)))
    go(remote(quarter(x), quarter(x), sem_tx.at[0, 0, 0], sem_tx.at[1, 0, 0], sib))

    lane = lax.broadcasted_iota(jnp.int32, (8, 128), 1)
    low = lane < 64
    sub = lax.broadcasted_iota(jnp.int32, (8, 128), 0)

    def pair(u0, u1, count):
        ev, od = [], []
        for i in range(count):
            v0 = u0[:, i * 128:(i + 1) * 128]
            v1 = u1[:, i * 128:(i + 1) * 128]
            ev.append(jnp.where(low, v0, pltpu.roll(v1, 64, 1)))
            od.append(jnp.where(low, pltpu.roll(v0, 64, 1), v1))
        return ev, od

    for q in range(4):
        arrived(tb.at[q], sem_wr.at[8, q])

    def build(p):
        for q in range(4):
            arrived(wr.at[p, q], sem_wr.at[p, q])
        code = tb[0, pl.ds(p, 1), :] + tb[1, pl.ds(p, 1), :] + tb[2, pl.ds(p, 1), :] + tb[3, pl.ds(p, 1), :]
        scale = tb[0, pl.ds(8 + p, 1), :] + tb[1, pl.ds(8 + p, 1), :] + tb[2, pl.ds(8 + p, 1), :] + tb[3, pl.ds(8 + p, 1), :]
        m = lax.broadcasted_iota(jnp.int32, (128, 128), 0).astype(F32)
        l = lax.broadcasted_iota(jnp.int32, (128, 128), 1)
        hit = jnp.logical_and(m == code, l < 64)
        factor = jnp.sum(jnp.where(hit, scale, 0.0), axis=1, keepdims=True)
        pick = jnp.where(hit, 1.0, 0.0).astype(BF)[:, :64]

        @pl.loop(0, 8)
        def _(n):
            lanes = pl.ds(mult(n * 512, 512), 512)
            slab = wr[p, :, :, lanes].reshape(64, 512)
            dense = jnp.dot(pick, slab, preferred_element_type=F32) * factor
            for q in range(4):
                for mat in range(2):
                    base = (q * 2 + mat) * 16
                    ev, od = pair(dense[base:base + 8], dense[base + 8:base + 16], 4)
                    for h, parts in ((0, ev), (1, od)):
                        panel[p, pl.ds(mult(q * 512 + h * 256 + n * 32, 32), 32), mat * 128:(mat + 1) * 128] = (
                            jnp.concatenate(parts, axis=0).astype(BF)
                        )

    EARLY = 3

    @pl.loop(0, EARLY)
    def _(p):
        build(p)

    for d in (1, 3, 2):
        xs = lax.rem(x + 4 - d, 4)
        for dz in range(4):
            arrived(block(xs, lax.rem(zl + 4 - dz, 4)), sem_tx.at[1, d, dz])
        go(remote(quarter(xs), quarter(xs), sem_tx.at[0, 0, d], sem_tx.at[1, 0, d], sib))
    siblane = mult((1 - core) * 1024, 1024)
    for d in (0, 1, 3, 2):
        xs = lax.rem(x + 4 - d, 4)
        arrived(x_all.at[pl.ds(mult(xs * 256, 256), 256), pl.ds(siblane, 1024)], sem_tx.at[1, 0, d])

    def product(p):
        def tokens_quarter(q):
            return jnp.dot(x_all[pl.ds(mult(q * 256, 256), 256), :], panel[p], preferred_element_type=F32)

        @pl.loop(0, 2)
        def _(i):
            bsend[p, pl.ds(mult(i * 256, 256), 256), :] = tokens_quarter(2 * (1 - b) + i).astype(BF)

        copy_b(p).start()

        @pl.loop(0, 2)
        def _(i):
            own[p, pl.ds(mult(i * 256, 256), 256), :] = tokens_quarter(2 * b + i)

    def copy_b(p):
        return remote(bsend.at[p], brecv.at[p], sem_b.at[0, p], sem_b.at[1, p], dev_b)

    def copy_z(p):
        return remote(zsend.at[p], zrecv.at[p], sem_z.at[0, p], sem_z.at[1, p], dev_z)

    def add_b(p):
        copy_b(p).wait_recv()
        away = pl.ds(mult((1 - zh) * 256, 256), 256)
        zsend[p] = (own[p, away, :] + brecv[p, away, :].astype(F32)).astype(BF)
        copy_z(p).start()
        keep = pl.ds(mult(zh * 256, 256), 256)
        own2[p] = own[p, keep, :] + brecv[p, keep, :].astype(F32)

    def add_z(p):
        copy_z(p).wait_recv()
        total = own2[p] + zrecv[p].astype(F32)
        gate = total[:, :128]
        hn[p] = (gate / (1.0 + jnp.exp(-gate)) * total[:, 128:]).astype(BF)

    def hpiece(s, c, q):
        off, width, _ = PIECES[s]
        return hid.at[pl.ds(mult(q * 256, 256), 256), pl.ds(mult(c * 896 + off, 128), width)]

    q_me = 2 * b + zh
    q_z = 2 * b + 1 - zh
    q_b = 2 * (1 - b) + zh
    q_bz = 2 * (1 - b) + 1 - zh

    def hcopy(s, n, q, dev):
        return remote(hpiece(s, core, q), hpiece(s, core, q), sem_hs.at[s, n], sem_hr.at[s, core * 4 + q], dev)

    def hstep_a(s):
        off, width, members = PIECES[s]
        first = (0, 4, 6)[s]
        parts = [hn[first + k] for k in range(width // 128)]
        nat = jnp.concatenate(parts, axis=1) if len(parts) > 1 else parts[0]
        order = p512[...] if s == 0 else order_matrix(width, members)
        hid[pl.ds(mult(q_me * 256, 256), 256), pl.ds(mult(core * 896 + off, 128), width)] = jnp.dot(
            nat, order, preferred_element_type=F32
        ).astype(BF)
        hcopy(s, 0, q_me, dev_z).start()
        hcopy(s, 1, q_me, dev_b).start()
        hcopy(s, 2, q_me, sib).start()

    def hstep_b(s):
        arrived(hpiece(s, core, q_z), sem_hr.at[s, core * 4 + q_z])
        hcopy(s, 3, q_z, dev_b).start()
        hcopy(s, 4, q_z, sib).start()

    def hstep_c(s):
        arrived(hpiece(s, core, q_b), sem_hr.at[s, core * 4 + q_b])
        hcopy(s, 5, q_b, sib).start()
        arrived(hpiece(s, core, q_bz), sem_hr.at[s, core * 4 + q_bz])
        hcopy(s, 6, q_bz, sib).start()

    def hstep_d(s):
        for q in range(4):
            arrived(hpiece(s, 1 - core, q), sem_hr.at[s, (1 - core) * 4 + q])

    def build_down():
        for side in range(2):
            arrived(td.at[side], sem_d.at[2, side])
            arrived(dr.at[side], sem_d.at[1, side])

        @pl.loop(0, 2)
        def _(side):
            code = td[side, 0:1, :]
            scale = td[side, 1:2, :]
            m = lax.broadcasted_iota(jnp.int32, (384, 128), 0)
            within = lax.rem(m, 8)
            piece = lax.rem(lax.div(m, 64), 3)
            members = jnp.where(piece == 0, 8, jnp.where(piece == 1, 4, 2))
            mm = (m - within + lax.rem(within, members)).astype(F32)
            hit = mm == code
            factor = jnp.sum(jnp.where(hit, scale, 0.0), axis=1, keepdims=True)
            pick = jnp.where(hit, 1.0, 0.0).astype(BF)[:, :112]

            @pl.loop(0, 4)
            def _(n):
                lanes = pl.ds(mult(n * 1024, 1024), 1024)
                dense = jnp.dot(pick, dr[side, :, lanes], preferred_element_type=F32) * factor
                for cc in range(2):
                    for s, (off, width, count) in enumerate(PIECES):
                        dup = 8 // count
                        for jp in range(4):
                            base = ((cc * 3 + s) * 8 + 2 * jp) * 8

                            def merged(r0):
                                u = dense[r0:r0 + 8]
                                tiles = [u[:, i * 128:(i + 1) * 128] for i in range(8)]
                                while len(tiles) > 8 // dup:
                                    half = 4 if len(tiles) == 8 and dup == 2 else None
                                    tiles = merge(tiles, dup)
                                return jnp.concatenate(tiles, axis=1)

                            def merge(tiles, dup):
                                res = []
                                for k in range(len(tiles) // dup):
                                    t = tiles[k * dup]
                                    for e in range(1, dup):
                                        t = jnp.where(lax.div(sub, count) == e, tiles[k * dup + e], t)
                                    res.append(t)
                                return res

                            ev, od = pair(merged(base), merged(base + 8), 8 // dup)
                            rows = 8 * count
                            for h, parts in ((0, ev), (1, od)):
                                start = mult(cc * 896 + off + h * (width // 2) + n * rows, 16)
                                wd[pl.ds(start, rows), pl.ds(mult(side * 512 + jp * 128, 128), 128)] = (
                                    jnp.concatenate(parts, axis=0) if len(parts) > 1 else parts[0]
                                ).astype(BF)

    @pl.loop(0, NCH + 3)
    def _(p):
        @pl.when(p < NCH)
        def _():
            @pl.when(p >= EARLY)
            def _():
                build(p)

            product(p)

        @pl.when(p == 7)
        def _():
            build_down()

        @pl.when(jnp.logical_and(p >= 1, p <= NCH))
        def _():
            add_b(p - 1)

        @pl.when(p >= 3)
        def _():
            add_z(p - 3)

        @pl.when(p == 6)
        def _():
            hstep_a(0)

        @pl.when(p == 8)
        def _():
            hstep_a(1)
            hstep_b(0)

        @pl.when(p == 9)
        def _():
            hstep_a(2)

    hstep_c(0)
    hstep_b(1)
    hstep_b(2)
    hstep_d(0)

    @pl.loop(0, 4)
    def _(q):
        rows = pl.ds(mult(q * 256, 256), 256)
        for n in range(2):
            cols = slice(n * 512, (n + 1) * 512)
            acc[rows, cols] = jnp.dot(hid[rows, 0:512], wd[0:512, cols], preferred_element_type=F32) + jnp.dot(
                hid[rows, 896:1408], wd[896:1408, cols], preferred_element_type=F32
            )

    for s in (1, 2):
        hstep_c(s)
    for s in (1, 2):
        hstep_d(s)

    def final(q, n):
        rows = pl.ds(mult(q * 256, 256), 256)
        cols = pl.ds(mult(n * 512, 512), 512)
        return (
            acc[rows, cols]
            + jnp.dot(hid[rows, 512:896], wd[512:896, cols], preferred_element_type=F32)
            + jnp.dot(hid[rows, 1408:1792], wd[1408:1792, cols], preferred_element_type=F32)
        )

    def copy_o1(i, d):
        return remote(o1s.at[i, d - 1], o1r.at[i, d - 1], sem_o1.at[0, i, d - 1], sem_o1.at[1, i, d - 1], xdev(d))

    def copy_o2(i, d):
        return remote(o2s.at[i, d - 1], o2r.at[i, d - 1], sem_o2.at[0, i, d - 1], sem_o2.at[1, i, d - 1], zdev(d))

    for i in range(2):
        n = 1 - kp if i == 0 else kp
        for d in (2, 1, 3):
            o1s[i, d - 1] = final(lax.rem(x + d, 4), n).astype(BF)
            copy_o1(i, d).start()
    mine = pl.ds(mult(x * 256, 256), 256)
    for i in range(2):
        n = 1 - kp if i == 0 else kp
        acc[mine, pl.ds(mult(n * 512, 512), 512)] = final(x, n)

    for i in range(2):
        n = 1 - kp if i == 0 else kp
        for d in (1, 3, 2):
            copy_o1(i, d).wait_recv()

        def summed(zs):
            r = pl.ds(mult(zs * 64, 64), 64)
            total = acc[pl.ds(mult(x * 256 + zs * 64, 64), 64), pl.ds(mult(n * 512, 512), 512)]
            for d in range(3):
                total = total + o1r[i, d, r, :].astype(F32)
            return total

        for d in (1, 3, 2):
            o2s[i, d - 1] = summed(lax.rem(zl + d, 4)).astype(BF)
            copy_o2(i, d).start()
        own3[i] = summed(zl)

    o3 = remote(o3s, out.at[pl.ds(mult(a * 64, 64), 64), :], sem_o3.at[0], sem_o3.at[1], dev_a)
    for i in range(2):
        for d in (1, 3, 2):
            copy_o2(i, d).wait_recv()
        total = own3[i]
        for d in range(3):
            total = total + o2r[i, d].astype(F32)
        if i == 0:
            o3s[...] = total.astype(BF)
            o3.start()
        else:
            out[pl.ds(mult(a * 64, 64), 64), :] = total.astype(BF)

    for copy in sends:
        copy.wait_send()

    @pl.loop(0, NCH)
    def _(p):
        copy_b(p).wait_send()
        copy_z(p).wait_send()

    for s in range(3):
        for n, q in ((0, q_me), (1, q_me), (2, q_me), (3, q_z), (4, q_z), (5, q_b), (6, q_bz)):
            hcopy(s, n, q, sib).wait_send()
    for i in range(2):
        for d in (1, 2, 3):
            copy_o1(i, d).wait_send()
            copy_o2(i, d).wait_send()
    o3.wait_send()
    arrived(out.at[pl.ds(mult((1 - a) * 64, 64), 64), :], sem_o3.at[1])


def per_device(
    tokens, gate_vals, gate_scales, gate_rows, up_vals, up_scales, up_rows, down_vals, down_scales, down_rows
):
    row = lax.axis_index("row")
    col = lax.axis_index("col")
    g = (row % 2) * 2 + (row // 2) % 2
    comb = jnp.concatenate([gate_vals.reshape(14, 8, 4096), up_vals.reshape(14, 8, 4096)], axis=1)
    draw = down_vals.transpose(1, 0, 2).reshape(112, 4096)

    lane = jnp.arange(128, dtype=jnp.int32)

    def chunked(gate, up):
        both = jnp.stack([gate.reshape(2, 7, 8), up.reshape(2, 7, 8)], axis=2).reshape(2, 7, 16)
        return jnp.pad(jnp.tile(both, (1, 1, 8)), ((0, 0), (0, 1), (0, 0)))

    where = chunked(gate_rows - row * 8, up_rows - row * 8) + 8 * (lane // 4)
    tabs = jnp.concatenate([where.astype(F32), chunked(gate_scales, up_scales)], axis=1)
    tabs = jnp.where(lane // 16 == g, tabs, 0.0)

    rel = down_rows - col * 28
    cc = rel // 14
    rr = rel - cc * 14
    piece = (rr >= 8).astype(jnp.int32) + (rr >= 12).astype(jnp.int32)
    rl = rr - jnp.where(piece == 0, 0, jnp.where(piece == 1, 8, 12))
    code = ((cc * 3 + piece) * 8 + jnp.arange(8, dtype=jnp.int32)[:, None]) * 8 + rl
    code = jnp.pad(code.T.reshape(1, 112).astype(F32), ((0, 0), (0, 16)), constant_values=-1.0)
    tabd = jnp.concatenate(
        [code, jnp.pad(down_scales.T.reshape(1, 112), ((0, 0), (0, 16))), jnp.zeros((6, 128), F32)], axis=0
    )

    vm = pl.BlockSpec(memory_space=pltpu.VMEM)
    hb = pl.BlockSpec(memory_space=pl.ANY)
    dma = pltpu.SemaphoreType.DMA
    return pl.pallas_call(
        kernel,
        out_shape=jax.ShapeDtypeStruct((128, 512), BF),
        in_specs=[vm, hb, hb, vm, vm],
        out_specs=vm,
        scratch_shapes=[
            pltpu.VMEM((1024, 2048), BF),
            pltpu.VMEM((128, 512), BF),
            pltpu.VMEM((512, 512), BF),
            pltpu.VMEM((NCH, 4, 16, 4096), BF),
            pltpu.VMEM((4, 16, 128), F32),
            pltpu.VMEM((2, 112, 4096), BF),
            pltpu.VMEM((2, 8, 128), F32),
            pltpu.VMEM((NCH, 2048, 256), BF),
            pltpu.VMEM((NCH, 512, 256), F32),
            pltpu.VMEM((NCH, 512, 256), BF),
            pltpu.VMEM((NCH, 512, 256), BF),
            pltpu.VMEM((NCH, 256, 256), F32),
            pltpu.VMEM((NCH, 256, 256), BF),
            pltpu.VMEM((NCH, 256, 256), BF),
            pltpu.VMEM((NCH, 256, 128), BF),
            pltpu.VMEM((1024, 1792), BF),
            pltpu.VMEM((1792, 1024), BF),
            pltpu.VMEM((1024, 1024), F32),
            pltpu.VMEM((2, 3, 256, 512), BF),
            pltpu.VMEM((2, 3, 256, 512), BF),
            pltpu.VMEM((2, 3, 64, 512), BF),
            pltpu.VMEM((2, 3, 64, 512), BF),
            pltpu.VMEM((2, 64, 512), F32),
            pltpu.VMEM((64, 512), BF),
            dma((2, 4)),
            dma((2, 4, 4)),
            dma((9, 3)),
            dma((9, 4)),
            dma((3, 2)),
            dma((2, NCH)),
            dma((2, NCH)),
            dma((3, 7)),
            dma((3, 8)),
            dma((2, 2, 3)),
            dma((2, 2, 3)),
            dma((2,)),
        ],
        compiler_params=pltpu.CompilerParams(
            collective_id=0, has_side_effects=True, vmem_limit_bytes=62 * 1024 * 1024
        ),
        name="gated_layer",
    )(tokens, comb, draw, tabs, tabd)


def solution(mesh):
    placed = (
        P("col", "row"),
        P("col", "row", None),
        P("col", "row"),
        P("col", "row"),
        P("col", "row", None),
        P("col", "row"),
        P("col", "row"),
        P("row", "col", None),
        P("row", "col"),
        P("row", "col"),
    )
    return jax.shard_map(
        per_device, mesh=mesh, in_specs=placed, out_specs=P("col", "row"), check_vma=False
    )
```

```python
import jax
import jax.numpy as jnp
from jax import lax
from jax.experimental import pallas as pl
from jax.experimental.pallas import tpu as pltpu
from jax.sharding import PartitionSpec as P

BF = jnp.bfloat16
F32 = jnp.float32
MESH = pl.DeviceIdType.MESH
NCH = 7
PIECES = ((0, 512, 8), (512, 256, 4), (768, 128, 2))


def mult(v, m):
    return pl.multiple_of(v, m)


def order_matrix(width, members):
    shift = members.bit_length() - 1
    k = lax.broadcasted_iota(jnp.int32, (1, width), 1)
    source = ((k & (members - 1)) << 6) + (((k >> shift) & 31) << 1) + (k >> (shift + 5))
    src = lax.broadcasted_iota(jnp.int32, (width, width), 0)
    return jnp.where(src == source, 1.0, 0.0).astype(BF)


def kernel(
    tok, graw, uraw, draw, grows, gscales, urows, uscales, drows, dscales, out,
    raw, comb, tabs, tabd, x_all, tst, p512, wr, tb, dr, td, panel,
    own, bsend, brecv, own2, zsend, zrecv, hn, hid, wd, acc,
    fars, farr, nears, nearr, o2s, o2r, own3, o3s,
    sem_raw, sem_t, sem_tx, sem_ws, sem_wr, sem_d, sem_b, sem_z, sem_hs, sem_hr, sem_far, sem_near, sem_o2, sem_o3,
):
    row = lax.axis_index("row")
    col = lax.axis_index("col")
    core = lax.rem(row, 2)
    y = lax.rem(lax.div(row, 2), 4)
    zh = lax.div(row, 8)
    x = lax.rem(col, 4)
    zl = lax.div(col, 4)
    b = lax.div(y, 2)
    kp = lax.rem(y, 2)
    a = lax.rem(lax.div(y + 1, 2), 2)
    g = core * 2 + kp
    sib = (row + 1 - 2 * core, col)
    row_a = row + 2 - 4 * kp
    dev_a = (row_a, col)
    dev_aa = (row_a + 1 - 2 * core, col)
    dev_b = (zh * 8 + (3 - y) * 2 + core, col)
    dev_z = ((1 - zh) * 8 + y * 2 + core, col)

    def xdev(d):
        return (row, zl * 4 + lax.rem(x + d, 4))

    def zdev(d):
        return (row, lax.rem(zl + d, 4) * 4 + x)

    def remote(src, dst, ss, rs, dev):
        return pltpu.make_async_remote_copy(
            src_ref=src, dst_ref=dst, send_sem=ss, recv_sem=rs, device_id=dev, device_id_type=MESH
        )

    def arrived(ref, sem):
        pltpu.make_async_copy(ref, ref, sem).wait()

    raw_copies = [pltpu.make_async_copy(src, raw.at[k], sem_raw.at[k]) for k, src in enumerate((graw, uraw))]
    for copy in raw_copies:
        copy.start()

    barrier = pltpu.get_barrier_semaphore()
    partners = [sib, dev_a, dev_aa, dev_b, dev_z] + [xdev(d) for d in (1, 2, 3)] + [zdev(d) for d in (1, 2, 3)]
    for dev in partners:
        pl.semaphore_signal(barrier, inc=1, device_id=dev, device_id_type=MESH)

    p512[...] = order_matrix(512, 8)
    tst[...] = jnp.dot(tok[...], p512[...], preferred_element_type=F32).astype(BF)
    myrow = mult((x * 4 + zl) * 64, 64)
    mylane = mult(core * 1024 + kp * 512, 512)
    corelane = mult(core * 1024, 1024)
    x_all[pl.ds(myrow, 64), pl.ds(mylane, 512)] = tst[pl.ds(mult(a * 64, 64), 64), :]

    pl.semaphore_wait(barrier, len(partners))

    sends = []

    def go(copy):
        copy.start()
        sends.append(copy)

    go(remote(tst.at[pl.ds(mult((1 - a) * 64, 64), 64), :],
              x_all.at[pl.ds(myrow, 64), pl.ds(mylane, 512)], sem_t.at[0, 0], sem_t.at[1, 0], dev_a))
    lane = lax.broadcasted_iota(jnp.int32, (8, 128), 1)
    sub = lax.broadcasted_iota(jnp.int32, (8, 128), 0)
    low = lane < 64

    jlane = lax.broadcasted_iota(jnp.int32, (8, 28), 1)
    jsub = lax.broadcasted_iota(jnp.int32, (8, 28), 0)
    for half in range(2):
        where = jnp.where((lane >> 4) == g, (lane >> 2) << 3, 0).astype(F32)
        scales = jnp.zeros((8, 128), F32)
        for mat, (rows_ref, scales_ref) in enumerate(((grows, gscales), (urows, uscales))):
            rel = (rows_ref[...] - row * 8).astype(F32)
            sc = scales_ref[...]
            for jj in range(2):
                mask = jlane == 14 * half + 2 * jsub + jj
                for k in range(4):
                    here = lane == 16 * g + 8 * mat + 4 * jj + k
                    v = jnp.sum(jnp.where(mask, rel[k:k + 1], 0.0), axis=1, keepdims=True)
                    w = jnp.sum(jnp.where(mask, sc[k:k + 1], 0.0), axis=1, keepdims=True)
                    where = where + jnp.where(here, v, 0.0)
                    scales = scales + jnp.where(here, w, 0.0)
        tabs[half, 0:8, :] = where
        tabs[half, 8:16, :] = scales
    rel = drows[...] - col * 28
    cc = jnp.where(rel >= 14, 1, 0)
    rr = rel - 14 * cc
    piece = jnp.where(rr >= 12, 2, jnp.where(rr >= 8, 1, 0))
    rl = rr - jnp.where(rr >= 12, 12, jnp.where(rr >= 8, 8, 0))
    j8 = lax.broadcasted_iota(jnp.int32, (8, 14), 0)
    code = ((((cc * 3 + piece) * 8 + j8) << 3) + rl).astype(F32)
    sc = dscales[...]
    cspread = jnp.zeros((8, 128), F32)
    sspread = jnp.zeros((8, 128), F32)
    for k in range(14):
        here = lane == 8 * k + sub
        cspread = cspread + jnp.where(here, code[:, k:k + 1], 0.0)
        sspread = sspread + jnp.where(here, sc[:, k:k + 1], 0.0)
    tabd[...] = jnp.where(
        sub == 0,
        jnp.where(lane < 112, jnp.sum(cspread, axis=0, keepdims=True), -1.0),
        jnp.sum(sspread, axis=0, keepdims=True),
    )

    wdests = ((dev_a, core), (dev_aa, 1 - core), (sib, 1 - core))

    def send_weights():
        for n, (dev, half) in enumerate(wdests):
            go(remote(tabs.at[half], tb.at[g], sem_ws.at[8, n], sem_wr.at[8, g], dev))
        pltpu.make_async_copy(tabs.at[core], tb.at[g], sem_wr.at[8, g]).start()
        for copy in raw_copies:
            copy.wait()

        @pl.loop(0, NCH)
        def _(p):
            for half in range(2):
                for k in range(2):
                    comb[half * NCH + p, 8 * k:8 * k + 8, :] = raw[k, pl.ds(2 * (half * NCH + p), 2)].reshape(8, 4096)
            for n, (dev, half) in enumerate(wdests):
                remote(comb.at[half * NCH + p], wr.at[p, g], sem_ws.at[p, n], sem_wr.at[p, g], dev).start()
            pltpu.make_async_copy(comb.at[core * NCH + p], wr.at[p, g], sem_wr.at[p, g]).start()

        go(remote(tabd, td.at[kp], sem_d.at[0, 0], sem_d.at[2, kp], dev_a))
        pltpu.make_async_copy(tabd, td.at[kp], sem_d.at[2, kp]).start()
        go(remote(draw, dr.at[kp], sem_d.at[0, 1], sem_d.at[1, kp], dev_a))
        pltpu.make_async_copy(draw, dr.at[kp], sem_d.at[1, kp]).start()

    def block(xs, zs):
        return x_all.at[pl.ds(mult((xs * 4 + zs) * 64, 64), 64), pl.ds(corelane, 1024)]

    def quarter(xs):
        return x_all.at[pl.ds(mult(xs * 256, 256), 256), pl.ds(corelane, 1024)]

    other = mult(core * 1024 + (1 - kp) * 512, 512)
    arrived(x_all.at[pl.ds(myrow, 64), pl.ds(other, 512)], sem_t.at[1, 0])
    for d in (1, 3, 2):
        go(remote(block(x, zl), block(x, zl), sem_t.at[0, d], sem_t.at[1, d], zdev(d)))

    def along_x(zs, dz):
        for d in (1, 3):
            go(remote(block(x, zs), block(x, zs), sem_tx.at[0, d, dz], sem_tx.at[1, d, dz], xdev(d)))

    def from_z(dz):
        zs = lax.rem(zl + 4 - dz, 4)
        arrived(block(x, zs), sem_t.at[1, dz])
        along_x(zs, dz)

    def onward(dz):
        d = 1 if dz % 2 == 0 else 3
        source = block(lax.rem(x + 4 - d, 4), lax.rem(zl + 4 - dz, 4))
        arrived(source, sem_tx.at[1, d, dz])
        go(remote(source, source, sem_tx.at[0, 2, dz], sem_tx.at[1, 2, dz], xdev(d)))

    along_x(zl, 0)
    send_weights()
    from_z(1)
    onward(0)
    from_z(3)
    onward(1)
    from_z(2)
    go(remote(quarter(x), quarter(x), sem_tx.at[0, 0, 0], sem_tx.at[1, 0, 0], sib))

    def pair(u0, u1, count):
        ev, od = [], []
        for i in range(count):
            v0 = u0[:, i * 128:(i + 1) * 128]
            v1 = u1[:, i * 128:(i + 1) * 128]
            ev.append(jnp.where(low, v0, pltpu.roll(v1, 64, 1)))
            od.append(jnp.where(low, pltpu.roll(v0, 64, 1), v1))
        return ev, od

    for q in range(4):
        arrived(tb.at[q], sem_wr.at[8, q])

    def build(p):
        for q in range(4):
            arrived(wr.at[p, q], sem_wr.at[p, q])
        code = tb[0, pl.ds(p, 1), :] + tb[1, pl.ds(p, 1), :] + tb[2, pl.ds(p, 1), :] + tb[3, pl.ds(p, 1), :]
        scale = tb[0, pl.ds(8 + p, 1), :] + tb[1, pl.ds(8 + p, 1), :] + tb[2, pl.ds(8 + p, 1), :] + tb[3, pl.ds(8 + p, 1), :]
        m = lax.broadcasted_iota(jnp.int32, (128, 128), 0).astype(F32)
        l = lax.broadcasted_iota(jnp.int32, (128, 128), 1)
        hit = jnp.logical_and(m == code, l < 64)
        factor = jnp.sum(jnp.where(hit, scale, 0.0), axis=1, keepdims=True)
        pick = jnp.where(hit, 1.0, 0.0).astype(BF)[:, :64]

        @pl.loop(0, 8)
        def _(n):
            lanes = pl.ds(mult(n * 512, 512), 512)
            slab = wr[p, :, :, lanes].reshape(64, 512)
            dense = jnp.dot(pick, slab, preferred_element_type=F32) * factor
            for q in range(4):
                for mat in range(2):
                    base = (q * 2 + mat) * 16
                    ev, od = pair(dense[base:base + 8], dense[base + 8:base + 16], 4)
                    for h, parts in ((0, ev), (1, od)):
                        panel[p, pl.ds(mult(q * 512 + h * 256 + n * 32, 32), 32), mat * 128:(mat + 1) * 128] = (
                            jnp.concatenate(parts, axis=0).astype(BF)
                        )

    EARLY = 3
    build(0)
    onward(3)
    onward(2)

    @pl.loop(1, EARLY)
    def _(p):
        build(p)

    for d in (1, 3, 2):
        xs = lax.rem(x + 4 - d, 4)
        waits = {1: (1, 3), 3: (0, 2), 2: (0, 1, 2, 3)}[d]
        for dz in waits:
            arrived(block(xs, lax.rem(zl + 4 - dz, 4)), sem_tx.at[1, d, dz])
        go(remote(quarter(xs), quarter(xs), sem_tx.at[0, 0, d], sem_tx.at[1, 0, d], sib))
    siblane = mult((1 - core) * 1024, 1024)
    for d in (0, 1, 3, 2):
        xs = lax.rem(x + 4 - d, 4)
        arrived(x_all.at[pl.ds(mult(xs * 256, 256), 256), pl.ds(siblane, 1024)], sem_tx.at[1, 0, d])

    def product(p):
        def tokens_quarter(q):
            return jnp.dot(x_all[pl.ds(mult(q * 256, 256), 256), :], panel[p], preferred_element_type=F32)

        def send_quarter(i):
            bsend[p, pl.ds(mult(i * 256, 256), 256), :] = tokens_quarter(2 * (1 - b) + i).astype(BF)
            copy_b(p, i).start()

        @pl.loop(0, 2)
        def _(k):
            send_quarter(lax.rem(1 - zh + k, 2))

        @pl.loop(0, 2)
        def _(i):
            own[p, pl.ds(mult(i * 256, 256), 256), :] = tokens_quarter(2 * b + i)

    def copy_b(p, i):
        rows = pl.ds(mult(i * 256, 256), 256)
        return remote(bsend.at[p, rows, :], brecv.at[p, rows, :], sem_b.at[0, p, i], sem_b.at[1, p, i], dev_b)

    def copy_z(p):
        return remote(zsend.at[p], zrecv.at[p], sem_z.at[0, p], sem_z.at[1, p], dev_z)

    def add_b(p):
        copy_b(p, 1 - zh).wait_recv()
        away = pl.ds(mult((1 - zh) * 256, 256), 256)
        zsend[p] = (own[p, away, :] + brecv[p, away, :].astype(F32)).astype(BF)
        copy_z(p).start()
        copy_b(p, zh).wait_recv()
        keep = pl.ds(mult(zh * 256, 256), 256)
        own2[p] = own[p, keep, :] + brecv[p, keep, :].astype(F32)

    def add_z(p):
        copy_z(p).wait_recv()
        total = own2[p] + zrecv[p].astype(F32)
        gate = total[:, :128]
        hn[p] = (gate / (1.0 + jnp.exp(-gate)) * total[:, 128:]).astype(BF)

    def hpiece(s, c, q):
        off, width, _ = PIECES[s]
        return hid.at[pl.ds(mult(q * 256, 256), 256), pl.ds(mult(c * 896 + off, 128), width)]

    q_me = 2 * b + zh
    q_z = 2 * b + 1 - zh
    q_b = 2 * (1 - b) + zh
    q_bz = 2 * (1 - b) + 1 - zh

    def hcopy(s, n, q, dev):
        return remote(hpiece(s, core, q), hpiece(s, core, q), sem_hs.at[s, n], sem_hr.at[s, core * 4 + q], dev)

    def hstep_a(s):
        off, width, members = PIECES[s]
        first = (0, 4, 6)[s]
        parts = [hn[first + k] for k in range(width // 128)]
        nat = jnp.concatenate(parts, axis=1) if len(parts) > 1 else parts[0]
        order = p512[...] if s == 0 else order_matrix(width, members)
        hid[pl.ds(mult(q_me * 256, 256), 256), pl.ds(mult(core * 896 + off, 128), width)] = jnp.dot(
            nat, order, preferred_element_type=F32
        ).astype(BF)
        hcopy(s, 0, q_me, dev_z).start()
        hcopy(s, 1, q_me, dev_b).start()
        hcopy(s, 2, q_me, sib).start()

    def hstep_b(s):
        arrived(hpiece(s, core, q_z), sem_hr.at[s, core * 4 + q_z])
        hcopy(s, 3, q_z, dev_b).start()
        hcopy(s, 4, q_z, sib).start()

    def hstep_c(s):
        arrived(hpiece(s, core, q_b), sem_hr.at[s, core * 4 + q_b])
        hcopy(s, 5, q_b, sib).start()
        arrived(hpiece(s, core, q_bz), sem_hr.at[s, core * 4 + q_bz])
        hcopy(s, 6, q_bz, sib).start()

    def hstep_d(s):
        for q in range(4):
            arrived(hpiece(s, 1 - core, q), sem_hr.at[s, (1 - core) * 4 + q])

    def build_down():
        for side in range(2):
            arrived(td.at[side], sem_d.at[2, side])
            arrived(dr.at[side], sem_d.at[1, side])

        @pl.loop(0, 2)
        def _(side):
            code = td[side, 0:1, :]
            scale = td[side, 1:2, :]
            m = lax.broadcasted_iota(jnp.int32, (384, 128), 0)
            within = m & 7
            sixes = m >> 6
            piece = jnp.where(sixes >= 3, sixes - 3, sixes)
            last = jnp.where(piece == 0, 7, jnp.where(piece == 1, 3, 1))
            mm = (m - within + (within & last)).astype(F32)
            hit = mm == code
            factor = jnp.sum(jnp.where(hit, scale, 0.0), axis=1, keepdims=True)
            pick = jnp.where(hit, 1.0, 0.0).astype(BF)[:, :112]

            @pl.loop(0, 4)
            def _(n):
                lanes = pl.ds(mult(n * 1024, 1024), 1024)
                dense = jnp.dot(pick, dr[side, :, lanes], preferred_element_type=F32) * factor
                for cc in range(2):
                    for s, (off, width, count) in enumerate(PIECES):
                        dup = 8 // count
                        for jp in range(4):
                            base = ((cc * 3 + s) * 8 + 2 * jp) * 8

                            def merged(r0):
                                u = dense[r0:r0 + 8]
                                tiles = [u[:, i * 128:(i + 1) * 128] for i in range(8)]
                                while len(tiles) > 8 // dup:
                                    tiles = merge(tiles, dup)
                                return jnp.concatenate(tiles, axis=1)

                            def merge(tiles, dup):
                                res = []
                                for k in range(len(tiles) // dup):
                                    t = tiles[k * dup]
                                    for e in range(1, dup):
                                        t = jnp.where((sub >> (count.bit_length() - 1)) == e, tiles[k * dup + e], t)
                                    res.append(t)
                                return res

                            ev, od = pair(merged(base), merged(base + 8), 8 // dup)
                            rows = 8 * count
                            for h, parts in ((0, ev), (1, od)):
                                start = mult(cc * 896 + off + h * (width // 2) + n * rows, 16)
                                wd[pl.ds(start, rows), pl.ds(mult(side * 512 + jp * 128, 128), 128)] = (
                                    jnp.concatenate(parts, axis=0) if len(parts) > 1 else parts[0]
                                ).astype(BF)

    @pl.loop(0, NCH + 3)
    def _(p):
        @pl.when(p < NCH)
        def _():
            @pl.when(p >= EARLY)
            def _():
                build(p)

            product(p)

        @pl.when(p == 7)
        def _():
            build_down()

        @pl.when(jnp.logical_and(p >= 1, p <= NCH))
        def _():
            add_b(p - 1)

        @pl.when(p >= 3)
        def _():
            add_z(p - 3)

        @pl.when(p == 6)
        def _():
            hstep_a(0)

        @pl.when(p == 8)
        def _():
            hstep_a(1)
            hstep_b(0)

        @pl.when(p == 9)
        def _():
            hstep_a(2)

    hstep_c(0)
    hstep_b(1)
    hstep_b(2)
    hstep_d(0)

    @pl.loop(0, 4)
    def _(q):
        rows = pl.ds(mult(q * 256, 256), 256)
        for n in range(2):
            cols = slice(n * 512, (n + 1) * 512)
            acc[rows, cols] = jnp.dot(hid[rows, 0:512], wd[0:512, cols], preferred_element_type=F32) + jnp.dot(
                hid[rows, 896:1408], wd[896:1408, cols], preferred_element_type=F32
            )

    for s in (1, 2):
        hstep_c(s)
    for s in (1, 2):
        hstep_d(s)

    def columns(i):
        return mult((1 - kp if i < 2 else kp) * 512 + (i % 2) * 256, 256)

    def final(q, i):
        rows = pl.ds(mult(q * 256, 256), 256)
        cols = pl.ds(columns(i), 256)
        return (
            acc[rows, cols]
            + jnp.dot(hid[rows, 512:896], wd[512:896, cols], preferred_element_type=F32)
            + jnp.dot(hid[rows, 1408:1792], wd[1408:1792, cols], preferred_element_type=F32)
        )

    def copy_far(i):
        return remote(fars.at[i], farr.at[i], sem_far.at[0, i], sem_far.at[1, i], xdev(1 if i % 2 == 0 else 3))

    def copy_near(d, i):
        k = d // 2
        return remote(nears.at[k, i], nearr.at[k, i], sem_near.at[0, k, i], sem_near.at[1, k, i], xdev(d))

    def copy_o2(i, d):
        return remote(o2s.at[i, d - 1], o2r.at[i, d - 1], sem_o2.at[0, i, d - 1], sem_o2.at[1, i, d - 1], zdev(d))

    def copy_o3(i):
        rows = pl.ds(mult(a * 64, 64), 64)
        return remote(o3s.at[i], out.at[rows, i * 256:(i + 1) * 256], sem_o3.at[0, i], sem_o3.at[1, i], dev_a)

    for i in range(4):
        fars[i] = final(lax.rem(x + 2, 4), i).astype(BF)
        copy_far(i).start()
    for i in range(4):
        d = 3 if i % 2 == 0 else 1
        nears[d // 2, i] = final(lax.rem(x + d, 4), i).astype(BF)
        copy_near(d, i).start()
    for i in range(4):
        d = 1 if i % 2 == 0 else 3
        mine = final(lax.rem(x + d, 4), i)
        copy_far(i).wait_recv()
        nears[d // 2, i] = (mine + farr[i].astype(F32)).astype(BF)
        copy_near(d, i).start()
    for i in range(4):
        acc[pl.ds(mult(x * 256, 256), 256), pl.ds(columns(i), 256)] = final(x, i)

    def finish(i):
        for d in (1, 3, 2):
            copy_o2(i, d).wait_recv()
        total = own3[i]
        for d in range(3):
            total = total + o2r[i, d].astype(F32)
        if i < 2:
            o3s[i] = total.astype(BF)
            copy_o3(i).start()
        else:
            out[pl.ds(mult(a * 64, 64), 64), (i - 2) * 256:(i - 1) * 256] = total.astype(BF)

    for i in range(4):
        for d in (1, 3):
            copy_near(d, i).wait_recv()

        def summed(zs):
            r = pl.ds(mult(zs * 64, 64), 64)
            total = acc[pl.ds(mult(x * 256 + zs * 64, 64), 64), pl.ds(columns(i), 256)]
            for k in range(2):
                total = total + nearr[k, i, r, :].astype(F32)
            return total

        for d in (2, 1, 3):
            o2s[i, d - 1] = summed(lax.rem(zl + d, 4)).astype(BF)
            copy_o2(i, d).start()
        own3[i] = summed(zl)
        if i >= 2:
            finish(i - 2)
    finish(2)
    finish(3)

    for copy in sends:
        copy.wait_send()

    @pl.loop(0, NCH)
    def _(p):
        for i in range(2):
            copy_b(p, i).wait_send()
        for n, (dev, half) in enumerate(wdests):
            remote(comb.at[half * NCH + p], wr.at[p, g], sem_ws.at[p, n], sem_wr.at[p, g], dev).wait_send()
        copy_z(p).wait_send()

    for s in range(3):
        for n, q in ((0, q_me), (1, q_me), (2, q_me), (3, q_z), (4, q_z), (5, q_b), (6, q_bz)):
            hcopy(s, n, q, sib).wait_send()
    for i in range(4):
        copy_far(i).wait_send()
        for d in (1, 3):
            copy_near(d, i).wait_send()
        for d in (1, 2, 3):
            copy_o2(i, d).wait_send()
    for i in range(2):
        copy_o3(i).wait_send()
        arrived(out.at[pl.ds(mult((1 - a) * 64, 64), 64), i * 256:(i + 1) * 256], sem_o3.at[1, i])


def per_device(
    tokens, gate_vals, gate_scales, gate_rows, up_vals, up_scales, up_rows, down_vals, down_scales, down_rows
):
    draw = down_vals.transpose(1, 0, 2).reshape(112, 4096)
    vm = pl.BlockSpec(memory_space=pltpu.VMEM)
    hb = pl.BlockSpec(memory_space=pl.ANY)
    dma = pltpu.SemaphoreType.DMA
    return pl.pallas_call(
        kernel,
        out_shape=jax.ShapeDtypeStruct((128, 512), BF),
        in_specs=[vm, hb, hb, hb] + [vm] * 6,
        out_specs=vm,
        scratch_shapes=[
            pltpu.VMEM((2, 28, 4, 4096), BF),
            pltpu.VMEM((14, 16, 4096), BF),
            pltpu.VMEM((2, 16, 128), F32),
            pltpu.VMEM((8, 128), F32),
            pltpu.VMEM((1024, 2048), BF),
            pltpu.VMEM((128, 512), BF),
            pltpu.VMEM((512, 512), BF),
            pltpu.VMEM((NCH, 4, 16, 4096), BF),
            pltpu.VMEM((4, 16, 128), F32),
            pltpu.VMEM((2, 112, 4096), BF),
            pltpu.VMEM((2, 8, 128), F32),
            pltpu.VMEM((NCH, 2048, 256), BF),
            pltpu.VMEM((NCH, 512, 256), F32),
            pltpu.VMEM((NCH, 512, 256), BF),
            pltpu.VMEM((NCH, 512, 256), BF),
            pltpu.VMEM((NCH, 256, 256), F32),
            pltpu.VMEM((NCH, 256, 256), BF),
            pltpu.VMEM((NCH, 256, 256), BF),
            pltpu.VMEM((NCH, 256, 128), BF),
            pltpu.VMEM((1024, 1792), BF),
            pltpu.VMEM((1792, 1024), BF),
            pltpu.VMEM((1024, 1024), F32),
            pltpu.VMEM((4, 256, 256), BF),
            pltpu.VMEM((4, 256, 256), BF),
            pltpu.VMEM((2, 4, 256, 256), BF),
            pltpu.VMEM((2, 4, 256, 256), BF),
            pltpu.VMEM((4, 3, 64, 256), BF),
            pltpu.VMEM((4, 3, 64, 256), BF),
            pltpu.VMEM((4, 64, 256), F32),
            pltpu.VMEM((2, 64, 256), BF),
            dma((2,)),
            dma((2, 4)),
            dma((2, 4, 4)),
            dma((9, 3)),
            dma((9, 4)),
            dma((3, 2)),
            dma((2, NCH, 2)),
            dma((2, NCH)),
            dma((3, 7)),
            dma((3, 8)),
            dma((2, 4)),
            dma((2, 2, 4)),
            dma((2, 4, 3)),
            dma((2, 2)),
        ],
        compiler_params=pltpu.CompilerParams(
            collective_id=0, has_side_effects=True, vmem_limit_bytes=62 * 1024 * 1024
        ),
        name="gated_layer",
    )(
        tokens, gate_vals, up_vals, draw, gate_rows.T, gate_scales.T, up_rows.T, up_scales.T, down_rows, down_scales
    )


def solution(mesh):
    placed = (
        P("col", "row"),
        P("col", "row", None),
        P("col", "row"),
        P("col", "row"),
        P("col", "row", None),
        P("col", "row"),
        P("col", "row"),
        P("row", "col", None),
        P("row", "col"),
        P("row", "col"),
    )
    return jax.shard_map(
        per_device, mesh=mesh, in_specs=placed, out_specs=P("col", "row"), check_vma=False
    )
```

```python
import jax
import jax.numpy as jnp
from jax import lax
from jax.experimental import pallas as pl
from jax.experimental.pallas import tpu as pltpu
from jax.sharding import PartitionSpec as P

BF = jnp.bfloat16
F32 = jnp.float32
MESH = pl.DeviceIdType.MESH
NCH = 7
PIECES = ((0, 512, 8), (512, 256, 4), (768, 128, 2))


def mult(v, m):
    return pl.multiple_of(v, m)


def order_matrix(width, members):
    shift = members.bit_length() - 1
    k = lax.broadcasted_iota(jnp.int32, (1, width), 1)
    source = ((k & (members - 1)) << 6) + (((k >> shift) & 31) << 1) + (k >> (shift + 5))
    src = lax.broadcasted_iota(jnp.int32, (width, width), 0)
    return jnp.where(src == source, 1.0, 0.0).astype(BF)


def kernel(
    tok, graw, uraw, draw, grows, gscales, urows, uscales, drows, dscales, out,
    raw, comb, tabs, tabd, x_all, tst, p512, wr, tb, dr, td, panel,
    own, bsend, brecv, own2, zsend, zrecv, hn, hid, wd, acc,
    fars, farr, nears, nearr, o2s, o2r, own3, o3s,
    sem_raw, sem_t, sem_zh, sem_xh, sem_sx, sem_tx, sem_ws, sem_wr, sem_d, sem_b, sem_z, sem_hs, sem_hr, sem_far, sem_near, sem_o2, sem_o3,
):
    row = lax.axis_index("row")
    col = lax.axis_index("col")
    core = lax.rem(row, 2)
    y = lax.rem(lax.div(row, 2), 4)
    zh = lax.div(row, 8)
    x = lax.rem(col, 4)
    zl = lax.div(col, 4)
    b = lax.div(y, 2)
    kp = lax.rem(y, 2)
    a = lax.rem(lax.div(y + 1, 2), 2)
    g = core * 2 + kp
    sib = (row + 1 - 2 * core, col)
    row_a = row + 2 - 4 * kp
    dev_a = (row_a, col)
    dev_aa = (row_a + 1 - 2 * core, col)
    dev_b = (zh * 8 + (3 - y) * 2 + core, col)
    dev_z = ((1 - zh) * 8 + y * 2 + core, col)

    def xdev(d):
        return (row, zl * 4 + lax.rem(x + d, 4))

    def zdev(d):
        return (row, lax.rem(zl + d, 4) * 4 + x)

    def remote(src, dst, ss, rs, dev):
        return pltpu.make_async_remote_copy(
            src_ref=src, dst_ref=dst, send_sem=ss, recv_sem=rs, device_id=dev, device_id_type=MESH
        )

    def arrived(ref, sem):
        pltpu.make_async_copy(ref, ref, sem).wait()

    raw_copies = [pltpu.make_async_copy(src, raw.at[k], sem_raw.at[k]) for k, src in enumerate((graw, uraw))]
    for copy in raw_copies:
        copy.start()

    barrier = pltpu.get_barrier_semaphore()
    partners = [sib, dev_a, dev_aa, dev_b, dev_z] + [xdev(d) for d in (1, 2, 3)] + [zdev(d) for d in (1, 2, 3)]
    for dev in partners:
        pl.semaphore_signal(barrier, inc=1, device_id=dev, device_id_type=MESH)

    p512[...] = order_matrix(512, 8)
    tst[...] = jnp.dot(tok[...], p512[...], preferred_element_type=F32).astype(BF)
    myrow = mult((x * 4 + zl) * 64, 64)
    mylane = mult(core * 1024 + kp * 512, 512)
    corelane = mult(core * 1024, 1024)
    x_all[pl.ds(myrow, 64), pl.ds(mylane, 512)] = tst[pl.ds(mult(a * 64, 64), 64), :]

    pl.semaphore_wait(barrier, len(partners))

    sends = []

    def go(copy):
        copy.start()
        sends.append(copy)

    go(remote(tst.at[pl.ds(mult((1 - a) * 64, 64), 64), :],
              x_all.at[pl.ds(myrow, 64), pl.ds(mylane, 512)], sem_t.at[0, 0], sem_t.at[1, 0], dev_a))
    other = mult(core * 1024 + (1 - kp) * 512, 512)

    def part(xs, zs, k):
        return x_all.at[pl.ds(mult((xs * 4 + zs) * 64, 64), 64), pl.ds(mylane if k == 0 else other, 512)]

    def spread_own(k):
        mine = part(x, zl, k)
        for d in (1, 3, 2):
            go(remote(mine, mine, sem_zh.at[0, k, d], sem_zh.at[1, k, d], zdev(d)))
        for d in (1, 3):
            go(remote(mine, mine, sem_xh.at[0, k, d], sem_xh.at[1, k, d], xdev(d)))

    spread_own(0)

    lane = lax.broadcasted_iota(jnp.int32, (8, 128), 1)
    sub = lax.broadcasted_iota(jnp.int32, (8, 128), 0)
    low = lane < 64

    jlane = lax.broadcasted_iota(jnp.int32, (8, 28), 1)
    jsub = lax.broadcasted_iota(jnp.int32, (8, 28), 0)
    for half in range(2):
        where = jnp.where((lane >> 4) == g, (lane >> 2) << 3, 0).astype(F32)
        scales = jnp.zeros((8, 128), F32)
        for mat, (rows_ref, scales_ref) in enumerate(((grows, gscales), (urows, uscales))):
            rel = (rows_ref[...] - row * 8).astype(F32)
            sc = scales_ref[...]
            for jj in range(2):
                mask = jlane == 14 * half + 2 * jsub + jj
                for k in range(4):
                    here = lane == 16 * g + 8 * mat + 4 * jj + k
                    v = jnp.sum(jnp.where(mask, rel[k:k + 1], 0.0), axis=1, keepdims=True)
                    w = jnp.sum(jnp.where(mask, sc[k:k + 1], 0.0), axis=1, keepdims=True)
                    where = where + jnp.where(here, v, 0.0)
                    scales = scales + jnp.where(here, w, 0.0)
        tabs[half, 0:8, :] = where
        tabs[half, 8:16, :] = scales
    rel = drows[...] - col * 28
    cc = jnp.where(rel >= 14, 1, 0)
    rr = rel - 14 * cc
    piece = jnp.where(rr >= 12, 2, jnp.where(rr >= 8, 1, 0))
    rl = rr - jnp.where(rr >= 12, 12, jnp.where(rr >= 8, 8, 0))
    j8 = lax.broadcasted_iota(jnp.int32, (8, 14), 0)
    code = ((((cc * 3 + piece) * 8 + j8) << 3) + rl).astype(F32)
    sc = dscales[...]
    cspread = jnp.zeros((8, 128), F32)
    sspread = jnp.zeros((8, 128), F32)
    for k in range(14):
        here = lane == 8 * k + sub
        cspread = cspread + jnp.where(here, code[:, k:k + 1], 0.0)
        sspread = sspread + jnp.where(here, sc[:, k:k + 1], 0.0)
    tabd[...] = jnp.where(
        sub == 0,
        jnp.where(lane < 112, jnp.sum(cspread, axis=0, keepdims=True), -1.0),
        jnp.sum(sspread, axis=0, keepdims=True),
    )

    wdests = ((dev_a, core), (dev_aa, 1 - core), (sib, 1 - core))

    def send_weights():
        for n, (dev, half) in enumerate(wdests):
            go(remote(tabs.at[half], tb.at[g], sem_ws.at[8, n], sem_wr.at[8, g], dev))
        pltpu.make_async_copy(tabs.at[core], tb.at[g], sem_wr.at[8, g]).start()
        for copy in raw_copies:
            copy.wait()

        @pl.loop(0, NCH)
        def _(p):
            for half in range(2):
                for k in range(2):
                    comb[half * NCH + p, 8 * k:8 * k + 8, :] = raw[k, pl.ds(2 * (half * NCH + p), 2)].reshape(8, 4096)
            for n, (dev, half) in enumerate(wdests):
                remote(comb.at[half * NCH + p], wr.at[p, g], sem_ws.at[p, n], sem_wr.at[p, g], dev).start()
            pltpu.make_async_copy(comb.at[core * NCH + p], wr.at[p, g], sem_wr.at[p, g]).start()

        go(remote(tabd, td.at[kp], sem_d.at[0, 0], sem_d.at[2, kp], dev_a))
        pltpu.make_async_copy(tabd, td.at[kp], sem_d.at[2, kp]).start()
        go(remote(draw, dr.at[kp], sem_d.at[0, 1], sem_d.at[1, kp], dev_a))
        pltpu.make_async_copy(draw, dr.at[kp], sem_d.at[1, kp]).start()

    def block(xs, zs):
        return x_all.at[pl.ds(mult((xs * 4 + zs) * 64, 64), 64), pl.ds(corelane, 1024)]

    def quarter(xs):
        return x_all.at[pl.ds(mult(xs * 256, 256), 256), pl.ds(corelane, 1024)]

    arrived(x_all.at[pl.ds(myrow, 64), pl.ds(other, 512)], sem_t.at[1, 0])
    spread_own(1)

    def along_x(zs, dz):
        for d in (1, 3):
            go(remote(block(x, zs), block(x, zs), sem_tx.at[0, d, dz], sem_tx.at[1, d, dz], xdev(d)))

    def from_z(dz):
        zs = lax.rem(zl + 4 - dz, 4)
        for k in range(2):
            arrived(part(x, zs, k), sem_zh.at[1, k, dz])
        along_x(zs, dz)

    def from_x(d, dz):
        xs, zs = lax.rem(x + 4 - d, 4), lax.rem(zl + 4 - dz, 4)
        if dz == 0 and d != 2:
            for k in range(2):
                arrived(part(xs, zs, k), sem_xh.at[1, k, d])
        else:
            arrived(block(xs, zs), sem_tx.at[1, d, dz])

    def onward(dz):
        d = 1 if dz % 2 == 0 else 3
        xs, zs = lax.rem(x + 4 - d, 4), lax.rem(zl + 4 - dz, 4)
        source = block(xs, zs)
        from_x(d, dz)
        go(remote(source, source, sem_tx.at[0, 2, dz], sem_tx.at[1, 2, dz], xdev(d)))

    send_weights()
    from_z(1)
    onward(0)
    from_z(3)
    onward(1)
    from_z(2)
    go(remote(quarter(x), quarter(x), sem_tx.at[0, 0, 0], sem_tx.at[1, 0, 0], sib))

    def pair(u0, u1, count):
        ev, od = [], []
        for i in range(count):
            v0 = u0[:, i * 128:(i + 1) * 128]
            v1 = u1[:, i * 128:(i + 1) * 128]
            ev.append(jnp.where(low, v0, pltpu.roll(v1, 64, 1)))
            od.append(jnp.where(low, pltpu.roll(v0, 64, 1), v1))
        return ev, od

    for q in range(4):
        arrived(tb.at[q], sem_wr.at[8, q])

    def build(p):
        for q in range(4):
            arrived(wr.at[p, q], sem_wr.at[p, q])
        code = tb[0, pl.ds(p, 1), :] + tb[1, pl.ds(p, 1), :] + tb[2, pl.ds(p, 1), :] + tb[3, pl.ds(p, 1), :]
        scale = tb[0, pl.ds(8 + p, 1), :] + tb[1, pl.ds(8 + p, 1), :] + tb[2, pl.ds(8 + p, 1), :] + tb[3, pl.ds(8 + p, 1), :]
        m = lax.broadcasted_iota(jnp.int32, (128, 128), 0).astype(F32)
        l = lax.broadcasted_iota(jnp.int32, (128, 128), 1)
        hit = jnp.logical_and(m == code, l < 64)
        factor = jnp.sum(jnp.where(hit, scale, 0.0), axis=1, keepdims=True)
        pick = jnp.where(hit, 1.0, 0.0).astype(BF)[:, :64]

        @pl.loop(0, 8)
        def _(n):
            lanes = pl.ds(mult(n * 512, 512), 512)
            slab = wr[p, :, :, lanes].reshape(64, 512)
            dense = jnp.dot(pick, slab, preferred_element_type=F32) * factor
            for q in range(4):
                for mat in range(2):
                    base = (q * 2 + mat) * 16
                    ev, od = pair(dense[base:base + 8], dense[base + 8:base + 16], 4)
                    for h, parts in ((0, ev), (1, od)):
                        panel[p, pl.ds(mult(q * 512 + h * 256 + n * 32, 32), 32), mat * 128:(mat + 1) * 128] = (
                            jnp.concatenate(parts, axis=0).astype(BF)
                        )

    EARLY = 3
    build(0)
    onward(3)
    onward(2)

    @pl.loop(1, EARLY)
    def _(p):
        build(p)

    for d, waits in ((1, (1, 3)), (3, (0, 2))):
        xs = lax.rem(x + 4 - d, 4)
        for dz in waits:
            from_x(d, dz)
        go(remote(quarter(xs), quarter(xs), sem_tx.at[0, 0, d], sem_tx.at[1, 0, d], sib))
    xs = lax.rem(x + 2, 4)
    for dz in (0, 1, 3, 2):
        from_x(2, dz)
        far = block(xs, lax.rem(zl + 4 - dz, 4))
        go(remote(far, far, sem_sx.at[0, dz], sem_sx.at[1, dz], sib))
    siblane = mult((1 - core) * 1024, 1024)
    for d in (0, 1, 3):
        xs = lax.rem(x + 4 - d, 4)
        arrived(x_all.at[pl.ds(mult(xs * 256, 256), 256), pl.ds(siblane, 1024)], sem_tx.at[1, 0, d])
    xs = lax.rem(x + 2, 4)
    for dz in range(4):
        zs = lax.rem(zl + 4 - dz, 4)
        arrived(x_all.at[pl.ds(mult((xs * 4 + zs) * 64, 64), 64), pl.ds(siblane, 1024)], sem_sx.at[1, dz])

    def product(p):
        def tokens_quarter(q):
            return jnp.dot(x_all[pl.ds(mult(q * 256, 256), 256), :], panel[p], preferred_element_type=F32)

        def send_quarter(i):
            bsend[p, pl.ds(mult(i * 256, 256), 256), :] = tokens_quarter(2 * (1 - b) + i).astype(BF)
            copy_b(p, i).start()

        @pl.loop(0, 2)
        def _(k):
            send_quarter(lax.rem(1 - zh + k, 2))

        @pl.loop(0, 2)
        def _(i):
            own[p, pl.ds(mult(i * 256, 256), 256), :] = tokens_quarter(2 * b + i)

    def copy_b(p, i):
        rows = pl.ds(mult(i * 256, 256), 256)
        return remote(bsend.at[p, rows, :], brecv.at[p, rows, :], sem_b.at[0, p, i], sem_b.at[1, p, i], dev_b)

    def copy_z(p):
        return remote(zsend.at[p], zrecv.at[p], sem_z.at[0, p], sem_z.at[1, p], dev_z)

    def add_b(p):
        copy_b(p, 1 - zh).wait_recv()
        away = pl.ds(mult((1 - zh) * 256, 256), 256)
        zsend[p] = (own[p, away, :] + brecv[p, away, :].astype(F32)).astype(BF)
        copy_z(p).start()
        copy_b(p, zh).wait_recv()
        keep = pl.ds(mult(zh * 256, 256), 256)
        own2[p] = own[p, keep, :] + brecv[p, keep, :].astype(F32)

    def add_z(p):
        copy_z(p).wait_recv()
        total = own2[p] + zrecv[p].astype(F32)
        gate = total[:, :128]
        hn[p] = (gate / (1.0 + jnp.exp(-gate)) * total[:, 128:]).astype(BF)

    def hpiece(s, c, q):
        off, width, _ = PIECES[s]
        return hid.at[pl.ds(mult(q * 256, 256), 256), pl.ds(mult(c * 896 + off, 128), width)]

    q_me = 2 * b + zh
    q_z = 2 * b + 1 - zh
    q_b = 2 * (1 - b) + zh
    q_bz = 2 * (1 - b) + 1 - zh

    def hcopy(s, n, q, dev):
        return remote(hpiece(s, core, q), hpiece(s, core, q), sem_hs.at[s, n], sem_hr.at[s, core * 4 + q], dev)

    def hstep_a(s):
        off, width, members = PIECES[s]
        first = (0, 4, 6)[s]
        parts = [hn[first + k] for k in range(width // 128)]
        nat = jnp.concatenate(parts, axis=1) if len(parts) > 1 else parts[0]
        order = p512[...] if s == 0 else order_matrix(width, members)
        hid[pl.ds(mult(q_me * 256, 256), 256), pl.ds(mult(core * 896 + off, 128), width)] = jnp.dot(
            nat, order, preferred_element_type=F32
        ).astype(BF)
        hcopy(s, 0, q_me, dev_z).start()
        hcopy(s, 1, q_me, dev_b).start()
        hcopy(s, 2, q_me, sib).start()

    def hstep_b(s):
        arrived(hpiece(s, core, q_z), sem_hr.at[s, core * 4 + q_z])
        hcopy(s, 3, q_z, dev_b).start()
        hcopy(s, 4, q_z, sib).start()

    def hstep_c(s):
        arrived(hpiece(s, core, q_b), sem_hr.at[s, core * 4 + q_b])
        hcopy(s, 5, q_b, sib).start()
        arrived(hpiece(s, core, q_bz), sem_hr.at[s, core * 4 + q_bz])
        hcopy(s, 6, q_bz, sib).start()

    def hstep_d(s):
        for q in range(4):
            arrived(hpiece(s, 1 - core, q), sem_hr.at[s, (1 - core) * 4 + q])

    def build_down():
        for side in range(2):
            arrived(td.at[side], sem_d.at[2, side])
            arrived(dr.at[side], sem_d.at[1, side])

        @pl.loop(0, 2)
        def _(side):
            code = td[side, 0:1, :]
            scale = td[side, 1:2, :]
            m = lax.broadcasted_iota(jnp.int32, (384, 128), 0)
            within = m & 7
            sixes = m >> 6
            piece = jnp.where(sixes >= 3, sixes - 3, sixes)
            last = jnp.where(piece == 0, 7, jnp.where(piece == 1, 3, 1))
            mm = (m - within + (within & last)).astype(F32)
            hit = mm == code
            factor = jnp.sum(jnp.where(hit, scale, 0.0), axis=1, keepdims=True)
            pick = jnp.where(hit, 1.0, 0.0).astype(BF)[:, :112]

            @pl.loop(0, 4)
            def _(n):
                lanes = pl.ds(mult(n * 1024, 1024), 1024)
                dense = jnp.dot(pick, dr[side, :, lanes], preferred_element_type=F32) * factor
                for cc in range(2):
                    for s, (off, width, count) in enumerate(PIECES):
                        dup = 8 // count
                        for jp in range(4):
                            base = ((cc * 3 + s) * 8 + 2 * jp) * 8

                            def merged(r0):
                                u = dense[r0:r0 + 8]
                                tiles = [u[:, i * 128:(i + 1) * 128] for i in range(8)]
                                while len(tiles) > 8 // dup:
                                    tiles = merge(tiles, dup)
                                return jnp.concatenate(tiles, axis=1)

                            def merge(tiles, dup):
                                res = []
                                for k in range(len(tiles) // dup):
                                    t = tiles[k * dup]
                                    for e in range(1, dup):
                                        t = jnp.where((sub >> (count.bit_length() - 1)) == e, tiles[k * dup + e], t)
                                    res.append(t)
                                return res

                            ev, od = pair(merged(base), merged(base + 8), 8 // dup)
                            rows = 8 * count
                            for h, parts in ((0, ev), (1, od)):
                                start = mult(cc * 896 + off + h * (width // 2) + n * rows, 16)
                                wd[pl.ds(start, rows), pl.ds(mult(side * 512 + jp * 128, 128), 128)] = (
                                    jnp.concatenate(parts, axis=0) if len(parts) > 1 else parts[0]
                                ).astype(BF)

    @pl.loop(0, NCH + 3)
    def _(p):
        @pl.when(p < NCH)
        def _():
            @pl.when(p >= EARLY)
            def _():
                build(p)

            product(p)

        @pl.when(p == 7)
        def _():
            build_down()

        @pl.when(jnp.logical_and(p >= 1, p <= NCH))
        def _():
            add_b(p - 1)

        @pl.when(p >= 3)
        def _():
            add_z(p - 3)

        @pl.when(p == 6)
        def _():
            hstep_a(0)

        @pl.when(p == 8)
        def _():
            hstep_a(1)
            hstep_b(0)

        @pl.when(p == 9)
        def _():
            hstep_a(2)

    hstep_c(0)
    hstep_b(1)
    hstep_b(2)
    hstep_d(0)

    @pl.loop(0, 4)
    def _(q):
        rows = pl.ds(mult(q * 256, 256), 256)
        for n in range(2):
            cols = slice(n * 512, (n + 1) * 512)
            acc[rows, cols] = jnp.dot(hid[rows, 0:512], wd[0:512, cols], preferred_element_type=F32) + jnp.dot(
                hid[rows, 896:1408], wd[896:1408, cols], preferred_element_type=F32
            )

    for s in (1, 2):
        hstep_c(s)
    for s in (1, 2):
        hstep_d(s)

    def columns(i):
        return mult((1 - kp if i < 2 else kp) * 512 + (i % 2) * 256, 256)

    def final(q, i):
        rows = pl.ds(mult(q * 256, 256), 256)
        cols = pl.ds(columns(i), 256)
        return (
            acc[rows, cols]
            + jnp.dot(hid[rows, 512:896], wd[512:896, cols], preferred_element_type=F32)
            + jnp.dot(hid[rows, 1408:1792], wd[1408:1792, cols], preferred_element_type=F32)
        )

    def copy_far(i):
        return remote(fars.at[i], farr.at[i], sem_far.at[0, i], sem_far.at[1, i], xdev(1 if i % 2 == 0 else 3))

    def copy_near(d, i):
        k = d // 2
        return remote(nears.at[k, i], nearr.at[k, i], sem_near.at[0, k, i], sem_near.at[1, k, i], xdev(d))

    def copy_o2(i, d):
        return remote(o2s.at[i, d - 1], o2r.at[i, d - 1], sem_o2.at[0, i, d - 1], sem_o2.at[1, i, d - 1], zdev(d))

    def copy_o3(i):
        rows = pl.ds(mult(a * 64, 64), 64)
        return remote(o3s.at[i], out.at[rows, i * 256:(i + 1) * 256], sem_o3.at[0, i], sem_o3.at[1, i], dev_a)

    for i in range(4):
        fars[i] = final(lax.rem(x + 2, 4), i).astype(BF)
        copy_far(i).start()
    for i in range(4):
        d = 3 if i % 2 == 0 else 1
        nears[d // 2, i] = final(lax.rem(x + d, 4), i).astype(BF)
        copy_near(d, i).start()
    for i in range(4):
        d = 1 if i % 2 == 0 else 3
        mine = final(lax.rem(x + d, 4), i)
        copy_far(i).wait_recv()
        nears[d // 2, i] = (mine + farr[i].astype(F32)).astype(BF)
        copy_near(d, i).start()
    for i in range(4):
        acc[pl.ds(mult(x * 256, 256), 256), pl.ds(columns(i), 256)] = final(x, i)

    def finish(i):
        for d in (1, 3, 2):
            copy_o2(i, d).wait_recv()
        total = own3[i]
        for d in range(3):
            total = total + o2r[i, d].astype(F32)
        if i < 2:
            o3s[i] = total.astype(BF)
            copy_o3(i).start()
        else:
            out[pl.ds(mult(a * 64, 64), 64), (i - 2) * 256:(i - 1) * 256] = total.astype(BF)

    for i in range(4):
        for d in (1, 3):
            copy_near(d, i).wait_recv()

        def summed(zs):
            r = pl.ds(mult(zs * 64, 64), 64)
            total = acc[pl.ds(mult(x * 256 + zs * 64, 64), 64), pl.ds(columns(i), 256)]
            for k in range(2):
                total = total + nearr[k, i, r, :].astype(F32)
            return total

        for d in (2, 1, 3):
            o2s[i, d - 1] = summed(lax.rem(zl + d, 4)).astype(BF)
            copy_o2(i, d).start()
        own3[i] = summed(zl)
        if i >= 2:
            finish(i - 2)
    finish(2)
    finish(3)

    for copy in sends:
        copy.wait_send()

    @pl.loop(0, NCH)
    def _(p):
        for i in range(2):
            copy_b(p, i).wait_send()
        for n, (dev, half) in enumerate(wdests):
            remote(comb.at[half * NCH + p], wr.at[p, g], sem_ws.at[p, n], sem_wr.at[p, g], dev).wait_send()
        copy_z(p).wait_send()

    for s in range(3):
        for n, q in ((0, q_me), (1, q_me), (2, q_me), (3, q_z), (4, q_z), (5, q_b), (6, q_bz)):
            hcopy(s, n, q, sib).wait_send()
    for i in range(4):
        copy_far(i).wait_send()
        for d in (1, 3):
            copy_near(d, i).wait_send()
        for d in (1, 2, 3):
            copy_o2(i, d).wait_send()
    for i in range(2):
        copy_o3(i).wait_send()
        arrived(out.at[pl.ds(mult((1 - a) * 64, 64), 64), i * 256:(i + 1) * 256], sem_o3.at[1, i])


def per_device(
    tokens, gate_vals, gate_scales, gate_rows, up_vals, up_scales, up_rows, down_vals, down_scales, down_rows
):
    draw = down_vals.transpose(1, 0, 2).reshape(112, 4096)
    vm = pl.BlockSpec(memory_space=pltpu.VMEM)
    hb = pl.BlockSpec(memory_space=pl.ANY)
    dma = pltpu.SemaphoreType.DMA
    return pl.pallas_call(
        kernel,
        out_shape=jax.ShapeDtypeStruct((128, 512), BF),
        in_specs=[vm, hb, hb, hb] + [vm] * 6,
        out_specs=vm,
        scratch_shapes=[
            pltpu.VMEM((2, 28, 4, 4096), BF),
            pltpu.VMEM((14, 16, 4096), BF),
            pltpu.VMEM((2, 16, 128), F32),
            pltpu.VMEM((8, 128), F32),
            pltpu.VMEM((1024, 2048), BF),
            pltpu.VMEM((128, 512), BF),
            pltpu.VMEM((512, 512), BF),
            pltpu.VMEM((NCH, 4, 16, 4096), BF),
            pltpu.VMEM((4, 16, 128), F32),
            pltpu.VMEM((2, 112, 4096), BF),
            pltpu.VMEM((2, 8, 128), F32),
            pltpu.VMEM((NCH, 2048, 256), BF),
            pltpu.VMEM((NCH, 512, 256), F32),
            pltpu.VMEM((NCH, 512, 256), BF),
            pltpu.VMEM((NCH, 512, 256), BF),
            pltpu.VMEM((NCH, 256, 256), F32),
            pltpu.VMEM((NCH, 256, 256), BF),
            pltpu.VMEM((NCH, 256, 256), BF),
            pltpu.VMEM((NCH, 256, 128), BF),
            pltpu.VMEM((1024, 1792), BF),
            pltpu.VMEM((1792, 1024), BF),
            pltpu.VMEM((1024, 1024), F32),
            pltpu.VMEM((4, 256, 256), BF),
            pltpu.VMEM((4, 256, 256), BF),
            pltpu.VMEM((2, 4, 256, 256), BF),
            pltpu.VMEM((2, 4, 256, 256), BF),
            pltpu.VMEM((4, 3, 64, 256), BF),
            pltpu.VMEM((4, 3, 64, 256), BF),
            pltpu.VMEM((4, 64, 256), F32),
            pltpu.VMEM((2, 64, 256), BF),
            dma((2,)),
            dma((2, 4)),
            dma((2, 2, 4)),
            dma((2, 2, 4)),
            dma((2, 4)),
            dma((2, 4, 4)),
            dma((9, 3)),
            dma((9, 4)),
            dma((3, 2)),
            dma((2, NCH, 2)),
            dma((2, NCH)),
            dma((3, 7)),
            dma((3, 8)),
            dma((2, 4)),
            dma((2, 2, 4)),
            dma((2, 4, 3)),
            dma((2, 2)),
        ],
        compiler_params=pltpu.CompilerParams(
            collective_id=0, has_side_effects=True, vmem_limit_bytes=62 * 1024 * 1024
        ),
        name="gated_layer",
    )(
        tokens, gate_vals, up_vals, draw, gate_rows.T, gate_scales.T, up_rows.T, up_scales.T, down_rows, down_scales
    )


def solution(mesh):
    placed = (
        P("col", "row"),
        P("col", "row", None),
        P("col", "row"),
        P("col", "row"),
        P("col", "row", None),
        P("col", "row"),
        P("col", "row"),
        P("row", "col", None),
        P("row", "col"),
        P("row", "col"),
    )
    return jax.shard_map(
        per_device, mesh=mesh, in_specs=placed, out_specs=P("col", "row"), check_vma=False
    )
```

```python
import jax
import jax.numpy as jnp
from jax import lax
from jax.experimental import pallas as pl
from jax.experimental.pallas import tpu as pltpu
from jax.sharding import PartitionSpec as P

BF = jnp.bfloat16
F32 = jnp.float32
MESH = pl.DeviceIdType.MESH
NCH = 7
PIECES = ((0, 512, 8), (512, 256, 4), (768, 128, 2))


def mult(v, m):
    return pl.multiple_of(v, m)


def order_matrix(width, members):
    shift = members.bit_length() - 1
    k = lax.broadcasted_iota(jnp.int32, (1, width), 1)
    source = ((k & (members - 1)) << 6) + (((k >> shift) & 31) << 1) + (k >> (shift + 5))
    src = lax.broadcasted_iota(jnp.int32, (width, width), 0)
    return jnp.where(src == source, 1.0, 0.0).astype(BF)


def kernel(
    tok, graw, uraw, draw, grows, gscales, urows, uscales, drows, dscales, out,
    raw, comb, tabs, tabd, x_all, tst, p512, wr, tb, dr, td, panel,
    own, bsend, brecv, own2, zsend, zrecv, hn, hid, wd, acc,
    fars, farr, nears, nearr, o2s, o2r, own3, o3s,
    sem_raw, sem_t, sem_zh, sem_xh, sem_sx, sem_tx, sem_ws, sem_wr, sem_d, sem_b, sem_z, sem_hs, sem_hr, sem_far, sem_near, sem_o2, sem_o3,
):
    row = lax.axis_index("row")
    col = lax.axis_index("col")
    core = lax.rem(row, 2)
    y = lax.rem(lax.div(row, 2), 4)
    zh = lax.div(row, 8)
    x = lax.rem(col, 4)
    zl = lax.div(col, 4)
    b = lax.div(y, 2)
    kp = lax.rem(y, 2)
    a = lax.rem(lax.div(y + 1, 2), 2)
    g = core * 2 + kp
    sib = (row + 1 - 2 * core, col)
    row_a = row + 2 - 4 * kp
    dev_a = (row_a, col)
    dev_aa = (row_a + 1 - 2 * core, col)
    dev_b = (zh * 8 + (3 - y) * 2 + core, col)
    dev_z = ((1 - zh) * 8 + y * 2 + core, col)

    def xdev(d):
        return (row, zl * 4 + lax.rem(x + d, 4))

    def zdev(d):
        return (row, lax.rem(zl + d, 4) * 4 + x)

    def remote(src, dst, ss, rs, dev):
        return pltpu.make_async_remote_copy(
            src_ref=src, dst_ref=dst, send_sem=ss, recv_sem=rs, device_id=dev, device_id_type=MESH
        )

    def arrived(ref, sem):
        pltpu.make_async_copy(ref, ref, sem).wait()

    raw_copies = [pltpu.make_async_copy(src, raw.at[k], sem_raw.at[k]) for k, src in enumerate((graw, uraw))]
    for copy in raw_copies:
        copy.start()

    barrier = pltpu.get_barrier_semaphore()
    partners = [sib, dev_a, dev_aa, dev_b, dev_z] + [xdev(d) for d in (1, 2, 3)] + [zdev(d) for d in (1, 2, 3)]
    for dev in partners:
        pl.semaphore_signal(barrier, inc=1, device_id=dev, device_id_type=MESH)

    p512[...] = order_matrix(512, 8)
    tst[...] = jnp.dot(tok[...], p512[...], preferred_element_type=F32).astype(BF)
    myrow = mult((x * 4 + zl) * 64, 64)
    mylane = mult(core * 1024 + kp * 512, 512)
    corelane = mult(core * 1024, 1024)
    x_all[pl.ds(myrow, 64), pl.ds(mylane, 512)] = tst[pl.ds(mult(a * 64, 64), 64), :]

    pl.semaphore_wait(barrier, len(partners))

    sends = []

    def go(copy):
        copy.start()
        sends.append(copy)

    go(remote(tst.at[pl.ds(mult((1 - a) * 64, 64), 64), :],
              x_all.at[pl.ds(myrow, 64), pl.ds(mylane, 512)], sem_t.at[0, 0], sem_t.at[1, 0], dev_a))
    other = mult(core * 1024 + (1 - kp) * 512, 512)

    def part(xs, zs, k):
        return x_all.at[pl.ds(mult((xs * 4 + zs) * 64, 64), 64), pl.ds(mylane if k == 0 else other, 512)]

    def spread_own(k):
        mine = part(x, zl, k)
        for d in (1, 3, 2):
            go(remote(mine, mine, sem_zh.at[0, k, d], sem_zh.at[1, k, d], zdev(d)))
        for d in (1, 3):
            go(remote(mine, mine, sem_xh.at[0, k, d], sem_xh.at[1, k, d], xdev(d)))

    spread_own(0)

    lane = lax.broadcasted_iota(jnp.int32, (8, 128), 1)
    sub = lax.broadcasted_iota(jnp.int32, (8, 128), 0)
    low = lane < 64

    jlane = lax.broadcasted_iota(jnp.int32, (8, 28), 1)
    jsub = lax.broadcasted_iota(jnp.int32, (8, 28), 0)
    for half in range(2):
        where = jnp.where((lane >> 4) == g, (lane >> 2) << 3, 0).astype(F32)
        scales = jnp.zeros((8, 128), F32)
        for mat, (rows_ref, scales_ref) in enumerate(((grows, gscales), (urows, uscales))):
            rel = (rows_ref[...] - row * 8).astype(F32)
            sc = scales_ref[...]
            for jj in range(2):
                mask = jlane == 14 * half + 2 * jsub + jj
                for k in range(4):
                    here = lane == 16 * g + 8 * mat + 4 * jj + k
                    v = jnp.sum(jnp.where(mask, rel[k:k + 1], 0.0), axis=1, keepdims=True)
                    w = jnp.sum(jnp.where(mask, sc[k:k + 1], 0.0), axis=1, keepdims=True)
                    where = where + jnp.where(here, v, 0.0)
                    scales = scales + jnp.where(here, w, 0.0)
        tabs[half, 0:8, :] = where
        tabs[half, 8:16, :] = scales
    rel = drows[...] - col * 28
    cc = jnp.where(rel >= 14, 1, 0)
    rr = rel - 14 * cc
    piece = jnp.where(rr >= 12, 2, jnp.where(rr >= 8, 1, 0))
    rl = rr - jnp.where(rr >= 12, 12, jnp.where(rr >= 8, 8, 0))
    j8 = lax.broadcasted_iota(jnp.int32, (8, 14), 0)
    code = ((((cc * 3 + piece) * 8 + j8) << 3) + rl).astype(F32)
    sc = dscales[...]
    cspread = jnp.zeros((8, 128), F32)
    sspread = jnp.zeros((8, 128), F32)
    for k in range(14):
        here = lane == 8 * k + sub
        cspread = cspread + jnp.where(here, code[:, k:k + 1], 0.0)
        sspread = sspread + jnp.where(here, sc[:, k:k + 1], 0.0)
    tabd[...] = jnp.where(
        sub == 0,
        jnp.where(lane < 112, jnp.sum(cspread, axis=0, keepdims=True), -1.0),
        jnp.sum(sspread, axis=0, keepdims=True),
    )

    wdests = ((dev_a, core), (dev_aa, 1 - core), (sib, 1 - core))

    def send_weights():
        for n, (dev, half) in enumerate(wdests):
            go(remote(tabs.at[half], tb.at[g], sem_ws.at[8, n], sem_wr.at[8, g], dev))
        pltpu.make_async_copy(tabs.at[core], tb.at[g], sem_wr.at[8, g]).start()
        for copy in raw_copies:
            copy.wait()

        @pl.loop(0, NCH)
        def _(p):
            for half in range(2):
                for k in range(2):
                    comb[half * NCH + p, 8 * k:8 * k + 8, :] = raw[k, pl.ds(2 * (half * NCH + p), 2)].reshape(8, 4096)
            for n, (dev, half) in enumerate(wdests):
                remote(comb.at[half * NCH + p], wr.at[p, g], sem_ws.at[p, n], sem_wr.at[p, g], dev).start()
            pltpu.make_async_copy(comb.at[core * NCH + p], wr.at[p, g], sem_wr.at[p, g]).start()

        go(remote(tabd, td.at[kp], sem_d.at[0, 0], sem_d.at[2, kp], dev_a))
        pltpu.make_async_copy(tabd, td.at[kp], sem_d.at[2, kp]).start()
        go(remote(draw, dr.at[kp], sem_d.at[0, 1], sem_d.at[1, kp], dev_a))
        pltpu.make_async_copy(draw, dr.at[kp], sem_d.at[1, kp]).start()

    def block(xs, zs):
        return x_all.at[pl.ds(mult((xs * 4 + zs) * 64, 64), 64), pl.ds(corelane, 1024)]

    def quarter(xs):
        return x_all.at[pl.ds(mult(xs * 256, 256), 256), pl.ds(corelane, 1024)]

    arrived(x_all.at[pl.ds(myrow, 64), pl.ds(other, 512)], sem_t.at[1, 0])
    spread_own(1)

    def along_x(zs, dz):
        for d in (1, 3):
            go(remote(block(x, zs), block(x, zs), sem_tx.at[0, d, dz], sem_tx.at[1, d, dz], xdev(d)))

    def from_z(dz):
        zs = lax.rem(zl + 4 - dz, 4)
        for k in range(2):
            arrived(part(x, zs, k), sem_zh.at[1, k, dz])
        along_x(zs, dz)

    def from_x(d, dz):
        xs, zs = lax.rem(x + 4 - d, 4), lax.rem(zl + 4 - dz, 4)
        if dz == 0 and d != 2:
            for k in range(2):
                arrived(part(xs, zs, k), sem_xh.at[1, k, d])
        else:
            arrived(block(xs, zs), sem_tx.at[1, d, dz])

    def onward(dz):
        d = 1 if dz % 2 == 0 else 3
        xs, zs = lax.rem(x + 4 - d, 4), lax.rem(zl + 4 - dz, 4)
        source = block(xs, zs)
        from_x(d, dz)
        go(remote(source, source, sem_tx.at[0, 2, dz], sem_tx.at[1, 2, dz], xdev(d)))

    send_weights()
    from_z(1)
    onward(0)
    from_z(3)
    onward(1)
    from_z(2)
    go(remote(quarter(x), quarter(x), sem_tx.at[0, 0, 0], sem_tx.at[1, 0, 0], sib))

    def pair(u0, u1, count):
        ev, od = [], []
        for i in range(count):
            v0 = u0[:, i * 128:(i + 1) * 128]
            v1 = u1[:, i * 128:(i + 1) * 128]
            ev.append(jnp.where(low, v0, pltpu.roll(v1, 64, 1)))
            od.append(jnp.where(low, pltpu.roll(v0, 64, 1), v1))
        return ev, od

    for q in range(4):
        arrived(tb.at[q], sem_wr.at[8, q])

    def build(p):
        for q in range(4):
            arrived(wr.at[p, q], sem_wr.at[p, q])
        code = tb[0, pl.ds(p, 1), :] + tb[1, pl.ds(p, 1), :] + tb[2, pl.ds(p, 1), :] + tb[3, pl.ds(p, 1), :]
        scale = tb[0, pl.ds(8 + p, 1), :] + tb[1, pl.ds(8 + p, 1), :] + tb[2, pl.ds(8 + p, 1), :] + tb[3, pl.ds(8 + p, 1), :]
        m = lax.broadcasted_iota(jnp.int32, (128, 128), 0).astype(F32)
        l = lax.broadcasted_iota(jnp.int32, (128, 128), 1)
        hit = jnp.logical_and(m == code, l < 64)
        factor = jnp.sum(jnp.where(hit, scale, 0.0), axis=1, keepdims=True)
        pick = jnp.where(hit, 1.0, 0.0).astype(BF)[:, :64]

        @pl.loop(0, 8)
        def _(n):
            lanes = pl.ds(mult(n * 512, 512), 512)
            slab = wr[p, :, :, lanes].reshape(64, 512)
            dense = jnp.dot(pick, slab, preferred_element_type=F32) * factor
            for q in range(4):
                for mat in range(2):
                    base = (q * 2 + mat) * 16
                    ev, od = pair(dense[base:base + 8], dense[base + 8:base + 16], 4)
                    for h, parts in ((0, ev), (1, od)):
                        panel[p, pl.ds(mult(q * 512 + h * 256 + n * 32, 32), 32), mat * 128:(mat + 1) * 128] = (
                            jnp.concatenate(parts, axis=0).astype(BF)
                        )

    EARLY = 1
    build(0)
    onward(3)
    onward(2)

    for d, waits in ((1, (1, 3)), (3, (0, 2))):
        xs = lax.rem(x + 4 - d, 4)
        for dz in waits:
            from_x(d, dz)
        go(remote(quarter(xs), quarter(xs), sem_tx.at[0, 0, d], sem_tx.at[1, 0, d], sib))
    xs = lax.rem(x + 2, 4)
    for dz in (0, 1, 3, 2):
        from_x(2, dz)
        far = block(xs, lax.rem(zl + 4 - dz, 4))
        go(remote(far, far, sem_sx.at[0, dz], sem_sx.at[1, dz], sib))
    siblane = mult((1 - core) * 1024, 1024)
    for d in (0, 1, 3):
        xs = lax.rem(x + 4 - d, 4)
        arrived(x_all.at[pl.ds(mult(xs * 256, 256), 256), pl.ds(siblane, 1024)], sem_tx.at[1, 0, d])
    xs = lax.rem(x + 2, 4)
    for dz in range(4):
        zs = lax.rem(zl + 4 - dz, 4)
        arrived(x_all.at[pl.ds(mult((xs * 4 + zs) * 64, 64), 64), pl.ds(siblane, 1024)], sem_sx.at[1, dz])

    def product(p):
        def tokens_quarter(q):
            return jnp.dot(x_all[pl.ds(mult(q * 256, 256), 256), :], panel[p], preferred_element_type=F32)

        def send_quarter(i):
            bsend[p, pl.ds(mult(i * 256, 256), 256), :] = tokens_quarter(2 * (1 - b) + i).astype(BF)
            copy_b(p, i).start()

        @pl.loop(0, 2)
        def _(k):
            send_quarter(lax.rem(1 - zh + k, 2))

        @pl.loop(0, 2)
        def _(i):
            own[p, pl.ds(mult(i * 256, 256), 256), :] = tokens_quarter(2 * b + i)

    def copy_b(p, i):
        rows = pl.ds(mult(i * 256, 256), 256)
        return remote(bsend.at[p, rows, :], brecv.at[p, rows, :], sem_b.at[0, p, i], sem_b.at[1, p, i], dev_b)

    def copy_z(p):
        return remote(zsend.at[p], zrecv.at[p], sem_z.at[0, p], sem_z.at[1, p], dev_z)

    def add_b(p):
        copy_b(p, 1 - zh).wait_recv()
        away = pl.ds(mult((1 - zh) * 256, 256), 256)
        zsend[p] = (own[p, away, :] + brecv[p, away, :].astype(F32)).astype(BF)
        copy_z(p).start()
        copy_b(p, zh).wait_recv()
        keep = pl.ds(mult(zh * 256, 256), 256)
        own2[p] = own[p, keep, :] + brecv[p, keep, :].astype(F32)

    def add_z(p):
        copy_z(p).wait_recv()
        total = own2[p] + zrecv[p].astype(F32)
        gate = total[:, :128]
        hn[p] = (gate / (1.0 + jnp.exp(-gate)) * total[:, 128:]).astype(BF)

    def hpiece(s, c, q):
        off, width, _ = PIECES[s]
        return hid.at[pl.ds(mult(q * 256, 256), 256), pl.ds(mult(c * 896 + off, 128), width)]

    q_me = 2 * b + zh
    q_z = 2 * b + 1 - zh
    q_b = 2 * (1 - b) + zh
    q_bz = 2 * (1 - b) + 1 - zh

    def hcopy(s, n, q, dev):
        return remote(hpiece(s, core, q), hpiece(s, core, q), sem_hs.at[s, n], sem_hr.at[s, core * 4 + q], dev)

    def hstep_a(s):
        off, width, members = PIECES[s]
        first = (0, 4, 6)[s]
        parts = [hn[first + k] for k in range(width // 128)]
        nat = jnp.concatenate(parts, axis=1) if len(parts) > 1 else parts[0]
        order = p512[...] if s == 0 else order_matrix(width, members)
        hid[pl.ds(mult(q_me * 256, 256), 256), pl.ds(mult(core * 896 + off, 128), width)] = jnp.dot(
            nat, order, preferred_element_type=F32
        ).astype(BF)
        hcopy(s, 0, q_me, dev_z).start()
        hcopy(s, 1, q_me, dev_b).start()
        hcopy(s, 2, q_me, sib).start()

    def hstep_b(s):
        arrived(hpiece(s, core, q_z), sem_hr.at[s, core * 4 + q_z])
        hcopy(s, 3, q_z, dev_b).start()
        hcopy(s, 4, q_z, sib).start()

    def hstep_c(s):
        arrived(hpiece(s, core, q_b), sem_hr.at[s, core * 4 + q_b])
        hcopy(s, 5, q_b, sib).start()
        arrived(hpiece(s, core, q_bz), sem_hr.at[s, core * 4 + q_bz])
        hcopy(s, 6, q_bz, sib).start()

    def hstep_d(s):
        for q in range(4):
            arrived(hpiece(s, 1 - core, q), sem_hr.at[s, (1 - core) * 4 + q])

    def build_down():
        for side in range(2):
            arrived(td.at[side], sem_d.at[2, side])
            arrived(dr.at[side], sem_d.at[1, side])

        @pl.loop(0, 2)
        def _(side):
            code = td[side, 0:1, :]
            scale = td[side, 1:2, :]
            m = lax.broadcasted_iota(jnp.int32, (384, 128), 0)
            within = m & 7
            sixes = m >> 6
            piece = jnp.where(sixes >= 3, sixes - 3, sixes)
            last = jnp.where(piece == 0, 7, jnp.where(piece == 1, 3, 1))
            mm = (m - within + (within & last)).astype(F32)
            hit = mm == code
            factor = jnp.sum(jnp.where(hit, scale, 0.0), axis=1, keepdims=True)
            pick = jnp.where(hit, 1.0, 0.0).astype(BF)[:, :112]

            @pl.loop(0, 4)
            def _(n):
                lanes = pl.ds(mult(n * 1024, 1024), 1024)
                dense = jnp.dot(pick, dr[side, :, lanes], preferred_element_type=F32) * factor
                for cc in range(2):
                    for s, (off, width, count) in enumerate(PIECES):
                        dup = 8 // count
                        for jp in range(4):
                            base = ((cc * 3 + s) * 8 + 2 * jp) * 8

                            def merged(r0):
                                u = dense[r0:r0 + 8]
                                tiles = [u[:, i * 128:(i + 1) * 128] for i in range(8)]
                                while len(tiles) > 8 // dup:
                                    tiles = merge(tiles, dup)
                                return jnp.concatenate(tiles, axis=1)

                            def merge(tiles, dup):
                                res = []
                                for k in range(len(tiles) // dup):
                                    t = tiles[k * dup]
                                    for e in range(1, dup):
                                        t = jnp.where((sub >> (count.bit_length() - 1)) == e, tiles[k * dup + e], t)
                                    res.append(t)
                                return res

                            ev, od = pair(merged(base), merged(base + 8), 8 // dup)
                            rows = 8 * count
                            for h, parts in ((0, ev), (1, od)):
                                start = mult(cc * 896 + off + h * (width // 2) + n * rows, 16)
                                wd[pl.ds(start, rows), pl.ds(mult(side * 512 + jp * 128, 128), 128)] = (
                                    jnp.concatenate(parts, axis=0) if len(parts) > 1 else parts[0]
                                ).astype(BF)

    @pl.loop(0, NCH + 3)
    def _(p):
        @pl.when(p < NCH)
        def _():
            product(p)

        @pl.when(p == 7)
        def _():
            build_down()

        @pl.when(jnp.logical_and(p >= 1, p <= NCH))
        def _():
            add_b(p - 1)

        @pl.when(p < NCH - 1)
        def _():
            build(p + 1)

        @pl.when(p >= 3)
        def _():
            add_z(p - 3)

        @pl.when(p == 6)
        def _():
            hstep_a(0)

        @pl.when(p == 8)
        def _():
            hstep_a(1)
            hstep_b(0)

        @pl.when(p == 9)
        def _():
            hstep_a(2)

    hstep_c(0)
    hstep_b(1)
    hstep_b(2)
    hstep_d(0)

    @pl.loop(0, 4)
    def _(q):
        rows = pl.ds(mult(q * 256, 256), 256)
        for n in range(2):
            cols = slice(n * 512, (n + 1) * 512)
            acc[rows, cols] = jnp.dot(hid[rows, 0:512], wd[0:512, cols], preferred_element_type=F32) + jnp.dot(
                hid[rows, 896:1408], wd[896:1408, cols], preferred_element_type=F32
            )

    for s in (1, 2):
        hstep_c(s)
    for s in (1, 2):
        hstep_d(s)

    def columns(i):
        return mult((1 - kp if i < 2 else kp) * 512 + (i % 2) * 256, 256)

    def final(q, i):
        rows = pl.ds(mult(q * 256, 256), 256)
        cols = pl.ds(columns(i), 256)
        return (
            acc[rows, cols]
            + jnp.dot(hid[rows, 512:896], wd[512:896, cols], preferred_element_type=F32)
            + jnp.dot(hid[rows, 1408:1792], wd[1408:1792, cols], preferred_element_type=F32)
        )

    def copy_far(i):
        return remote(fars.at[i], farr.at[i], sem_far.at[0, i], sem_far.at[1, i], xdev(1 if i % 2 == 0 else 3))

    def copy_near(d, i):
        k = d // 2
        return remote(nears.at[k, i], nearr.at[k, i], sem_near.at[0, k, i], sem_near.at[1, k, i], xdev(d))

    def copy_o2(i, d):
        return remote(o2s.at[i, d - 1], o2r.at[i, d - 1], sem_o2.at[0, i, d - 1], sem_o2.at[1, i, d - 1], zdev(d))

    def copy_o3(i):
        rows = pl.ds(mult(a * 64, 64), 64)
        return remote(o3s.at[i], out.at[rows, i * 256:(i + 1) * 256], sem_o3.at[0, i], sem_o3.at[1, i], dev_a)

    for i in range(4):
        fars[i] = final(lax.rem(x + 2, 4), i).astype(BF)
        copy_far(i).start()
    for i in range(4):
        d = 3 if i % 2 == 0 else 1
        nears[d // 2, i] = final(lax.rem(x + d, 4), i).astype(BF)
        copy_near(d, i).start()
    for i in range(4):
        d = 1 if i % 2 == 0 else 3
        mine = final(lax.rem(x + d, 4), i)
        copy_far(i).wait_recv()
        nears[d // 2, i] = (mine + farr[i].astype(F32)).astype(BF)
        copy_near(d, i).start()
    for i in range(4):
        acc[pl.ds(mult(x * 256, 256), 256), pl.ds(columns(i), 256)] = final(x, i)

    def finish(i):
        for d in (1, 3, 2):
            copy_o2(i, d).wait_recv()
        total = own3[i]
        for d in range(3):
            total = total + o2r[i, d].astype(F32)
        if i < 2:
            o3s[i] = total.astype(BF)
            copy_o3(i).start()
        else:
            out[pl.ds(mult(a * 64, 64), 64), (i - 2) * 256:(i - 1) * 256] = total.astype(BF)

    for i in range(4):
        for d in (1, 3):
            copy_near(d, i).wait_recv()

        def summed(zs):
            r = pl.ds(mult(zs * 64, 64), 64)
            total = acc[pl.ds(mult(x * 256 + zs * 64, 64), 64), pl.ds(columns(i), 256)]
            for k in range(2):
                total = total + nearr[k, i, r, :].astype(F32)
            return total

        for d in (2, 1, 3):
            o2s[i, d - 1] = summed(lax.rem(zl + d, 4)).astype(BF)
            copy_o2(i, d).start()
        own3[i] = summed(zl)
        if i >= 2:
            finish(i - 2)
    finish(2)
    finish(3)

    for copy in sends:
        copy.wait_send()

    @pl.loop(0, NCH)
    def _(p):
        for i in range(2):
            copy_b(p, i).wait_send()
        for n, (dev, half) in enumerate(wdests):
            remote(comb.at[half * NCH + p], wr.at[p, g], sem_ws.at[p, n], sem_wr.at[p, g], dev).wait_send()
        copy_z(p).wait_send()

    for s in range(3):
        for n, q in ((0, q_me), (1, q_me), (2, q_me), (3, q_z), (4, q_z), (5, q_b), (6, q_bz)):
            hcopy(s, n, q, sib).wait_send()
    for i in range(4):
        copy_far(i).wait_send()
        for d in (1, 3):
            copy_near(d, i).wait_send()
        for d in (1, 2, 3):
            copy_o2(i, d).wait_send()
    for i in range(2):
        copy_o3(i).wait_send()
        arrived(out.at[pl.ds(mult((1 - a) * 64, 64), 64), i * 256:(i + 1) * 256], sem_o3.at[1, i])


def per_device(
    tokens, gate_vals, gate_scales, gate_rows, up_vals, up_scales, up_rows, down_vals, down_scales, down_rows
):
    draw = down_vals.transpose(1, 0, 2).reshape(112, 4096)
    vm = pl.BlockSpec(memory_space=pltpu.VMEM)
    hb = pl.BlockSpec(memory_space=pl.ANY)
    dma = pltpu.SemaphoreType.DMA
    return pl.pallas_call(
        kernel,
        out_shape=jax.ShapeDtypeStruct((128, 512), BF),
        in_specs=[vm, hb, hb, hb] + [vm] * 6,
        out_specs=vm,
        scratch_shapes=[
            pltpu.VMEM((2, 28, 4, 4096), BF),
            pltpu.VMEM((14, 16, 4096), BF),
            pltpu.VMEM((2, 16, 128), F32),
            pltpu.VMEM((8, 128), F32),
            pltpu.VMEM((1024, 2048), BF),
            pltpu.VMEM((128, 512), BF),
            pltpu.VMEM((512, 512), BF),
            pltpu.VMEM((NCH, 4, 16, 4096), BF),
            pltpu.VMEM((4, 16, 128), F32),
            pltpu.VMEM((2, 112, 4096), BF),
            pltpu.VMEM((2, 8, 128), F32),
            pltpu.VMEM((NCH, 2048, 256), BF),
            pltpu.VMEM((NCH, 512, 256), F32),
            pltpu.VMEM((NCH, 512, 256), BF),
            pltpu.VMEM((NCH, 512, 256), BF),
            pltpu.VMEM((NCH, 256, 256), F32),
            pltpu.VMEM((NCH, 256, 256), BF),
            pltpu.VMEM((NCH, 256, 256), BF),
            pltpu.VMEM((NCH, 256, 128), BF),
            pltpu.VMEM((1024, 1792), BF),
            pltpu.VMEM((1792, 1024), BF),
            pltpu.VMEM((1024, 1024), F32),
            pltpu.VMEM((4, 256, 256), BF),
            pltpu.VMEM((4, 256, 256), BF),
            pltpu.VMEM((2, 4, 256, 256), BF),
            pltpu.VMEM((2, 4, 256, 256), BF),
            pltpu.VMEM((4, 3, 64, 256), BF),
            pltpu.VMEM((4, 3, 64, 256), BF),
            pltpu.VMEM((4, 64, 256), F32),
            pltpu.VMEM((2, 64, 256), BF),
            dma((2,)),
            dma((2, 4)),
            dma((2, 2, 4)),
            dma((2, 2, 4)),
            dma((2, 4)),
            dma((2, 4, 4)),
            dma((9, 3)),
            dma((9, 4)),
            dma((3, 2)),
            dma((2, NCH, 2)),
            dma((2, NCH)),
            dma((3, 7)),
            dma((3, 8)),
            dma((2, 4)),
            dma((2, 2, 4)),
            dma((2, 4, 3)),
            dma((2, 2)),
        ],
        compiler_params=pltpu.CompilerParams(
            collective_id=0, has_side_effects=True, vmem_limit_bytes=62 * 1024 * 1024
        ),
        name="gated_layer",
    )(
        tokens, gate_vals, up_vals, draw, gate_rows.T, gate_scales.T, up_rows.T, up_scales.T, down_rows, down_scales
    )


def solution(mesh):
    placed = (
        P("col", "row"),
        P("col", "row", None),
        P("col", "row"),
        P("col", "row"),
        P("col", "row", None),
        P("col", "row"),
        P("col", "row"),
        P("row", "col", None),
        P("row", "col"),
        P("row", "col"),
    )
    return jax.shard_map(
        per_device, mesh=mesh, in_specs=placed, out_specs=P("col", "row"), check_vma=False
    )
```
